256 devices in a mesh: step: 64 (over z, y, core), space: 4 (over x).
Axes of the slice: x: 4, y: 4, z: 8, core: 2. Of those that a mesh axis runs over, the one named last changes fastest.
Arguments:
- guesses: float32 [64, 64, 4, 2560], P('step', None, None, 'space'), may hold values from -6 to 6
- noise: float32 [64, 64, 4, 2560], P('step', None, None, 'space'), may hold values from -6 to 6
- timesteps: int32 [64, 2], P('step'), may hold values from 1 to 999, as said below
- conv_first: bfloat16 [3, 256, 576], replicated, may hold values from -0.15625 to 0.15625
- conv_second: bfloat16 [3, 64, 2304], replicated, may hold values from -0.078125 to 0.078125
- time_weight: float32 [64, 256], replicated, may hold values from -0.75 to 0.75
Outputs:
- states: float32 [64, 64, 4, 2560], P('step', None, None, 'space')
- changes: float32 [64], P('step')
The draws below stay inside these ranges and needn't reach their ends.
Inputs may be any that keep to these rules, and one draw needn't show every extreme that they name: Row k holds the timesteps before and after step k: the first entry of row 0 is 999, the second entry of the last row is 1, each row's second entry equals the next row's first, and the first entries fall strictly.
All inputs are finite; a program needn't handle non-finite values.
Results may differ from the reference program's by a relative error of at most 0.0019.
Values may be sent and summed in bfloat16 or wider, within the bound.
A program may use at most 64 MiB of HBM per device.

```python
import math
import jax
import jax.numpy as jnp
from jax import lax

C = 64
HID = 256
FRAMES = 4
COLS = 80
STEPS = 64
ROWS = 32


def draw_timesteps(key, part):
    order = jax.random.permutation(jax.random.fold_in(key, 7), 997)
    middle = (order[:STEPS - 1] + 2).astype(jnp.int32)
    middle = -jnp.sort(-middle)
    chain = jnp.concatenate([jnp.array([999], jnp.int32), middle, jnp.array([1], jnp.int32)])
    return jnp.stack([chain[:-1], chain[1:]], axis=1)


def levels(own_key, dims, shards, low, largest):
    gain, own = 1.0, jax.random.fold_in(own_key, 6)
    for position, shards_of in shards:
        steps = jnp.exp(jax.random.uniform(jax.random.fold_in(own, position), (shards_of,), jnp.float32, low / len(shards), largest / len(shards)))
        gain = gain * jnp.repeat(steps, dims[position] // shards_of).reshape([-1 if axis == position else 1 for axis in range(len(dims))])
    return gain


def bell_draw(stream_key, shape, width, most, pieces=(), kind=jnp.bfloat16):
    values = jax.random.normal(stream_key, shape, jnp.float32) * width
    if len(pieces) > 0:
        values = levels(stream_key, shape, pieces, -0.22, 0.18) * values
    return jnp.clip(values, min=-most, max=most).astype(kind)


def setup_inputs(seed: int = 0) -> dict:
    seeds = jax.random.split(jax.random.key(seed), 7)
    guesses = bell_draw(seeds[0], (STEPS, C, FRAMES, ROWS * COLS), 1.0, 6.0, ((0, 64), (3, 4)), jnp.float32)
    noise = bell_draw(seeds[1], (STEPS, C, FRAMES, ROWS * COLS), 1.0, 6.0, ((0, 64), (3, 4)), jnp.float32)
    timesteps = draw_timesteps(jax.random.fold_in(seeds[6], 71), 0)
    conv_first = bell_draw(seeds[3], (3, HID, 9 * C), (27 * C) ** -0.5, 0.15625)
    conv_second = bell_draw(seeds[4], (3, C, 9 * HID), (27 * HID) ** -0.5, 0.078125)
    time_weight = bell_draw(seeds[5], (C, HID), C ** -0.5, 0.75, (), jnp.float32)
    return {"guesses": guesses, "noise": noise, "timesteps": timesteps, "conv_first": conv_first, "conv_second": conv_second, "time_weight": time_weight}


def plan(timestep):
    scaled = timestep.astype(jnp.float32) / 1000.0
    return -(0.1 * scaled + 9.95 * scaled * scaled)

def coefficients(timestep_pair):
    log_from = plan(timestep_pair[0])
    log_to = plan(timestep_pair[1])
    half_gap = 0.5 * (log_to - log_from)
    decay_gain = jnp.expm1(half_gap)
    remain_from = -jnp.expm1(log_from)
    remain_to = -jnp.expm1(log_to)
    ratio_term = -jnp.expm1(log_from - log_to)
    noise_gain = -jnp.exp(half_gap) * jnp.sqrt(remain_from) + remain_to * jnp.exp(-half_gap) / jnp.sqrt(remain_from)
    spread_gain = jnp.sqrt(remain_to / remain_from * ratio_term)
    return (decay_gain, noise_gain, spread_gain)

def time_embed(timestep, time_weight):
    half_count = C // 2
    frequency = jnp.exp(-math.log(10000.0) * jnp.arange(half_count, dtype=jnp.float32) / half_count)
    angles = timestep.astype(jnp.float32) * frequency
    features = jnp.concatenate([jnp.sin(angles), jnp.cos(angles)])
    return jnp.dot(features, time_weight, preferred_element_type=jnp.float32, precision=lax.Precision.HIGHEST)

def convolve(volume, weight):
    out_count = weight.shape[1]
    in_count = weight.shape[2] // 9
    kernel = weight.astype(jnp.float32).reshape(3, out_count, 3, 3, in_count).transpose(1, 4, 0, 2, 3)
    result = lax.conv_general_dilated(volume[None], kernel, (1, 1, 1), ((1, 1), (1, 1), (1, 1)), dimension_numbers=('NCDHW', 'OIDHW', 'NCDHW'), precision=lax.Precision.HIGHEST)
    return result[0]

def drift_of(latent, noise_step, timestep_pair, conv_first, conv_second, time_weight):
    decay_gain, noise_gain, spread_gain = coefficients(timestep_pair)
    temb = time_embed(timestep_pair[0], time_weight)
    rounded = lax.optimization_barrier(latent.astype(jnp.bfloat16)).astype(jnp.float32)
    volume = rounded.reshape(C, FRAMES, ROWS, COLS)
    preact = convolve(volume, conv_first) + temb[:, None, None, None]
    hidden = lax.optimization_barrier(jax.nn.silu(preact).astype(jnp.bfloat16)).astype(jnp.float32)
    predicted = convolve(hidden, conv_second).reshape(C, FRAMES, ROWS * COLS)
    return decay_gain * latent + noise_gain * predicted + spread_gain * noise_step

def picard_sweep(trajectory, noise, timesteps, conv_first, conv_second, time_weight):

    def advance(running, inputs):
        latent, noise_step, timestep_pair = inputs
        drift = drift_of(latent, noise_step, timestep_pair, conv_first, conv_second, time_weight)
        reached = running + drift
        return (reached, (running, reached))
    _, (entering, reached) = lax.scan(advance, trajectory[0], (trajectory, noise, timesteps))
    return (entering, reached)

def reference(guesses, noise, timesteps, conv_first, conv_second, time_weight):
    entering_one, reached_one = picard_sweep(guesses, noise, timesteps, conv_first, conv_second, time_weight)
    entering_two, reached_two = picard_sweep(entering_one, noise, timesteps, conv_first, conv_second, time_weight)
    difference = reached_two - reached_one
    changes = jnp.sqrt(lax.optimization_barrier(jnp.mean(difference * difference, axis=(1, 2, 3))))
    return (reached_two, changes)
```

```python
import math

import jax
import jax.numpy as jnp
from jax import lax
from jax.experimental import pallas as pl
from jax.experimental.pallas import tpu as pltpu
from jax.sharding import PartitionSpec as P

C = 64
HID = 256
COLS = 80
FRAMES = 4
BF = jnp.bfloat16
F32 = jnp.float32
MESH = pl.DeviceIdType.MESH

PX = 640
OWN = 256
EXT = OWN + PX + 256
Q0 = 128
NQ = 896
HALF = C // 2
TILES = HALF // 8 * (PX // 128)
ALL_TILES = FRAMES * TILES
BLOCKS = PX // 128
CHUNK = 256


def plan(timestep):
    scaled = timestep.astype(F32) / 1000.0
    return -(0.1 * scaled + 9.95 * scaled * scaled)


def coefficients(timestep_pair):
    log_from = plan(timestep_pair[0])
    log_to = plan(timestep_pair[1])
    half_gap = 0.5 * (log_to - log_from)
    decay_gain = jnp.expm1(half_gap)
    remain_from = -jnp.expm1(log_from)
    remain_to = -jnp.expm1(log_to)
    ratio_term = -jnp.expm1(log_from - log_to)
    noise_gain = -jnp.exp(half_gap) * jnp.sqrt(remain_from) + remain_to * jnp.exp(
        -half_gap
    ) / jnp.sqrt(remain_from)
    spread_gain = jnp.sqrt(remain_to / remain_from * ratio_term)
    return jnp.stack([decay_gain, noise_gain, spread_gain])


def time_embed(timestep, time_weight):
    half_count = C // 2
    frequency = jnp.exp(-math.log(10000.0) * jnp.arange(half_count, dtype=F32) / half_count)
    angles = timestep.astype(F32) * frequency
    features = jnp.concatenate([jnp.sin(angles), jnp.cos(angles)])
    return jnp.dot(
        features, time_weight, preferred_element_type=F32, precision=lax.Precision.HIGHEST
    )


def make_kernel(chips, columns_of_space, cell_count):
    slots = -(-ALL_TILES // chips)

    def kernel(
        coef, temb, y_ref, n_ref, w1_ref, w2_ref, out_ref, chg_ref,
        ent, ebf, xc, hid, grp, w1s, w2s,
        st, pb, cs, rx, tx, px, eo, dump, ssq,
        halo_send, halo_recv, pair_send, pair_recv, cs_send, rx_recv, tx_send, px_recv,
        eo_send, ent_recv, ssq_send, ssq_recv,
    ):
        step = lax.axis_index("step")
        space = lax.axis_index("space")
        chip = step // 2
        core = step - 2 * chip
        other = 1 - core
        partner = 2 * chip + other
        anchor = step == 0
        mine_rows = pl.ds(pl.multiple_of(core * HALF, HALF), HALF)
        other_rows = pl.ds(pl.multiple_of(other * HALF, HALF), HALF)

        for s in range(2):
            for f in range(FRAMES):
                ebf[s, f, :, 0:OWN] = jnp.zeros((C, OWN), BF)
                ebf[s, f, :, OWN + PX : EXT] = jnp.zeros((C, OWN), BF)

        barrier = pltpu.get_barrier_semaphore()

        @pl.loop(1, chips)
        def _(d):
            target = lax.rem(chip + d, chips)
            pl.semaphore_signal(
                barrier, inc=1, device_id={"step": 2 * target + core}, device_id_type=MESH
            )

        pl.semaphore_signal(barrier, inc=1, device_id={"step": partner}, device_id_type=MESH)
        for d in range(1, columns_of_space):
            pl.semaphore_signal(
                barrier,
                inc=1,
                device_id={"space": lax.rem(space + d, columns_of_space)},
                device_id_type=MESH,
            )

        lane = lax.broadcasted_iota(jnp.int32, (1, EXT), 1)
        column = lax.rem(lane + (4 * COLS - OWN % COLS), COLS)
        not_last = column != COLS - 1
        not_first = column != 0

        def frame_of(ref, f):
            return jnp.concatenate(
                [ref[pl.ds(b * FRAMES + f, C, stride=BLOCKS * FRAMES), :] for b in range(BLOCKS)],
                axis=1,
            )

        def halo_copies(s, f):
            right = pltpu.make_async_remote_copy(
                src_ref=ebf.at[s, f, :, pl.ds(OWN + PX - 256, 256)],
                dst_ref=ebf.at[s, f, :, pl.ds(0, 256)],
                send_sem=halo_send.at[s, f, 0],
                recv_sem=halo_recv.at[s, f, 0],
                device_id={"space": lax.rem(space + 1, columns_of_space)},
                device_id_type=MESH,
            )
            left = pltpu.make_async_remote_copy(
                src_ref=ebf.at[s, f, :, pl.ds(OWN, 256)],
                dst_ref=ebf.at[s, f, :, pl.ds(OWN + PX, 256)],
                send_sem=halo_send.at[s, f, 1],
                recv_sem=halo_recv.at[s, f, 1],
                device_id={"space": lax.rem(space + columns_of_space - 1, columns_of_space)},
                device_id_type=MESH,
            )
            return right, left

        def halo_start(s, f):
            right, left = halo_copies(s, f)

            @pl.when(space < columns_of_space - 1)
            def _():
                right.start()

            @pl.when(space > 0)
            def _():
                left.start()

        def halo_wait(s, f):
            right, left = halo_copies(s, f)

            @pl.when(space > 0)
            def _():
                right.wait_recv()

            @pl.when(space < columns_of_space - 1)
            def _():
                left.wait_recv()

        def halo_done(s, f):
            right, left = halo_copies(s, f)

            @pl.when(space < columns_of_space - 1)
            def _():
                right.wait_send()

            @pl.when(space > 0)
            def _():
                left.wait_send()

        def im2col(s, f):
            halo_wait(s, f)
            whole = ebf[s, f]
            zero = jnp.zeros_like(whole)
            shifted = (jnp.where(not_last, whole, zero), whole, jnp.where(not_first, whole, zero))
            for b in range(3):
                for c in range(3):
                    start = Q0 + COLS * (b - 1) + (c - 1)
                    row = f * 9 * C + (b * 3 + c) * C
                    xc[row : row + C, :] = shifted[c][:, start : start + NQ]

        def conv_one(f):
            low, high = max(f - 1, 0), min(f + 2, FRAMES)
            first = low - f + 1
            weights = w1s[:, 9 * C * first : 9 * C * (first + high - low)]
            for n in range(0, NQ, CHUNK):
                m = min(n + CHUNK, NQ)
                value = jnp.dot(
                    weights, xc[low * 9 * C : high * 9 * C, n:m], preferred_element_type=F32
                )
                value = value + temb[...]
                value = value / (1.0 + jnp.exp(-value))
                if n + Q0 < OWN:
                    place = lax.broadcasted_iota(jnp.int32, (1, m - n), 1) + (n + Q0)
                    value = jnp.where((place >= OWN) | (space > 0), value, 0.0)
                if m + Q0 > OWN + PX:
                    place = lax.broadcasted_iota(jnp.int32, (1, m - n), 1) + (n + Q0)
                    value = jnp.where(
                        (place < OWN + PX) | (space < columns_of_space - 1), value, 0.0
                    )
                hid[f * HID : (f + 1) * HID, n:m] = value.astype(BF)

        def conv_two(f):
            low, high = max(f - 1, 0), min(f + 2, FRAMES)
            first = low - f + 1
            weights = w2s[:, HID * first : HID * (first + high - low)]
            for n in range(0, NQ, CHUNK):
                m = min(n + CHUNK, NQ)
                grp[:, n:m] = jnp.dot(
                    weights, hid[low * HID : high * HID, n:m], preferred_element_type=F32
                )
            masks = (not_last[:, Q0 : Q0 + NQ], None, not_first[:, Q0 : Q0 + NQ])
            total = None
            for b in range(3):
                for c in range(3):
                    tap = b * 3 + c
                    value = grp[tap * C : (tap + 1) * C, :]
                    if masks[c] is not None:
                        value = jnp.where(masks[c], value, 0.0)
                    start = OWN - Q0 + COLS * (b - 1) + (c - 1)
                    value = pltpu.roll(value, (NQ - start) % NQ, 1)[:, :PX]
                    total = value if total is None else total + value
            return total

        def pair_copy(s, f):
            return pltpu.make_async_remote_copy(
                src_ref=st.at[s, f, other_rows, :],
                dst_ref=pb.at[s, f],
                send_sem=pair_send.at[s, f],
                recv_sem=pair_recv.at[s, f],
                device_id={"step": partner},
                device_id_type=MESH,
            )

        def drift(s, f):
            latent = ent[s, f]
            value = coef[0] * latent + coef[1] * conv_two(f) + coef[2] * frame_of(n_ref, f)
            st[s, f] = value + jnp.where(anchor, latent, 0.0)
            pair_copy(s, f).start()

        def chip_sum(s, f):
            pair_copy(s, f).wait_recv()
            total = st[s, f, mine_rows, :] + pb[s, f]
            for r in range(HALF // 8):
                for b in range(BLOCKS):
                    cs[s, f * TILES + r * BLOCKS + b] = total[
                        8 * r : 8 * r + 8, 128 * b : 128 * b + 128
                    ]

            @pl.loop(f * TILES, (f + 1) * TILES)
            def _(g):
                slot = g // chips
                owner = g - slot * chips

                @pl.when(owner != chip)
                def _():
                    pltpu.make_async_remote_copy(
                        src_ref=cs.at[s, g],
                        dst_ref=rx.at[s, slot, chip],
                        send_sem=cs_send.at[s],
                        recv_sem=rx_recv.at[s, slot],
                        device_id={"step": 2 * owner + core},
                        device_id_type=MESH,
                    ).start()

                @pl.when(owner == chip)
                def _():
                    pltpu.make_async_copy(
                        cs.at[s, g], rx.at[s, slot, chip], rx_recv.at[s, slot]
                    ).start()
                    pltpu.make_async_copy(cs.at[s, g], dump.at[s, slot, 0], cs_send.at[s]).start()

        def own(s, slot):
            tile = slot * chips + chip

            def work():
                pltpu.make_async_copy(rx.at[s, slot], rx.at[s, slot], rx_recv.at[s, slot]).wait()
                running = jnp.zeros((8, 128), F32)
                for q in range(chips):
                    tx[s, slot, q] = running
                    running = running + rx[s, slot, q]
                frame = tile // TILES

                @pl.loop(1, chips)
                def _(d):
                    target = lax.rem(chip + d, chips)
                    pltpu.make_async_remote_copy(
                        src_ref=tx.at[s, slot, target],
                        dst_ref=px.at[s, tile],
                        send_sem=tx_send.at[s, slot],
                        recv_sem=px_recv.at[s, frame],
                        device_id={"step": 2 * target + core},
                        device_id_type=MESH,
                    ).start()

                pltpu.make_async_copy(
                    tx.at[s, slot, chip], px.at[s, tile], px_recv.at[s, frame]
                ).start()
                pltpu.make_async_copy(
                    tx.at[s, slot, chip], dump.at[s, slot, 1], tx_send.at[s, slot]
                ).start()

            if (slot + 1) * chips <= ALL_TILES:
                work()
            else:
                pl.when(tile < ALL_TILES)(work)

        def own_done(s, slot):
            def work():
                pltpu.make_async_copy(tx.at[s, slot], tx.at[s, slot], tx_send.at[s, slot]).wait()

            if (slot + 1) * chips <= ALL_TILES:
                work()
            else:
                pl.when(slot * chips + chip < ALL_TILES)(work)

        def enter_copy(s, f):
            return pltpu.make_async_remote_copy(
                src_ref=eo.at[s, f],
                dst_ref=ent.at[s + 1, f, mine_rows, :],
                send_sem=eo_send.at[s, f],
                recv_sem=ent_recv.at[s, f],
                device_id={"step": partner},
                device_id_type=MESH,
            )

        def enter(s, f):
            tiles = px.at[s, pl.ds(f * TILES, TILES)]
            pltpu.make_async_copy(tiles, tiles, px_recv.at[s, f]).wait()
            before = jnp.concatenate(
                [
                    jnp.concatenate(
                        [px[s, f * TILES + r * BLOCKS + b] for b in range(BLOCKS)], axis=1
                    )
                    for r in range(HALF // 8)
                ],
                axis=0,
            )
            first = jnp.where(core == 0, st[s, f, mine_rows, :], pb[s, f])
            after = before + first
            eo[s, f] = jnp.where(core == 0, after, before)
            enter_copy(s, f).start()
            ent[s + 1, f, mine_rows, :] = jnp.where(core == 0, before, after)

        def entered(s, f):
            copy = enter_copy(s, f)
            pltpu.make_async_copy(
                ent.at[s + 1, f, other_rows, :], ent.at[s + 1, f, other_rows, :], ent_recv.at[s, f]
            ).wait()

            @pl.when(anchor)
            def _():
                ent[s + 1, f] = ent[0, f]

        def latent_out(s, f):
            ebf[s, f, :, OWN : OWN + PX] = ent[s, f].astype(BF)
            halo_start(s, f)

        for f in range(FRAMES):
            ent[0, f] = frame_of(y_ref, f)
        for a in range(3):
            for tap in range(9):
                w2s[tap * C : (tap + 1) * C, a * HID : (a + 1) * HID] = w2_ref[
                    a, :, tap * HID : (tap + 1) * HID
                ]
        w1s[...] = jnp.concatenate([w1_ref[0], w1_ref[1], w1_ref[2]], axis=1)

        pl.semaphore_wait(barrier, chips + columns_of_space - 1)
        for f in range(FRAMES):
            latent_out(0, f)

        for s in range(2):
            im2col(s, 0)
            im2col(s, 1)
            conv_one(0)
            im2col(s, 2)
            conv_one(1)
            drift(s, 0)
            im2col(s, 3)
            conv_one(2)
            chip_sum(s, 0)
            drift(s, 1)
            conv_one(3)
            chip_sum(s, 1)
            drift(s, 2)
            chip_sum(s, 2)
            drift(s, 3)
            chip_sum(s, 3)
            for slot in range(slots):
                own(s, slot)
            for f in range(FRAMES):
                enter(s, f)
            square = None
            for f in range(FRAMES):
                entered(s, f)
                if s == 0:
                    latent_out(1, f)
                else:
                    keep = jnp.where(anchor, 0.0, 1.0)
                    reached = keep * ent[2, f] + st[1, f]
                    change = reached - (keep * ent[1, f] + st[0, f])
                    change = change * change
                    for r in range(C // 8):
                        for b in range(BLOCKS):
                            part = change[8 * r : 8 * r + 8, 128 * b : 128 * b + 128]
                            square = part if square is None else square + part
                    for b in range(BLOCKS):
                        out_ref[pl.ds(b * FRAMES + f, C, stride=BLOCKS * FRAMES), :] = reached[
                            :, 128 * b : 128 * b + 128
                        ]
            if s == 1:
                ssq[0] = square

        def ssq_copy(d):
            return pltpu.make_async_remote_copy(
                src_ref=ssq.at[0],
                dst_ref=ssq.at[columns_of_space + 1 - d],
                send_sem=ssq_send.at[d - 1],
                recv_sem=ssq_recv.at[columns_of_space - 1 - d],
                device_id={"space": lax.rem(space + d, columns_of_space)},
                device_id_type=MESH,
            )

        for d in range(1, columns_of_space):
            ssq_copy(d).start()

        for s in range(2):
            for f in range(FRAMES):
                halo_done(s, f)
                pair_copy(s, f).wait_send()
                enter_copy(s, f).wait_send()
            pltpu.make_async_copy(cs.at[s], cs.at[s], cs_send.at[s]).wait()
            for slot in range(slots):
                own_done(s, slot)

        for d in range(1, columns_of_space):
            ssq_copy(d).wait_send()
        for d in range(1, columns_of_space):
            ssq_copy(columns_of_space - d).wait_recv()
        total = None
        for x in range(columns_of_space):
            part = None
            for d in range(columns_of_space):
                place = 0 if d == 0 else d + 1
                term = jnp.where(lax.rem(space + d, columns_of_space) == x, ssq[place], 0.0)
                part = term if part is None else part + term
            total = part if total is None else total + part
        mean = jnp.sum(total) / cell_count
        chg_ref[...] = jnp.sqrt(jnp.full((8, 128), mean, F32))

    scratch = [
        pltpu.VMEM((3, FRAMES, C, PX), F32),
        pltpu.VMEM((2, FRAMES, C, EXT), BF),
        pltpu.VMEM((FRAMES * 9 * C, NQ), BF),
        pltpu.VMEM((FRAMES * HID, NQ), BF),
        pltpu.VMEM((9 * C, NQ), F32),
        pltpu.VMEM((HID, 27 * C), BF),
        pltpu.VMEM((9 * C, 3 * HID), BF),
        pltpu.VMEM((2, FRAMES, C, PX), F32),
        pltpu.VMEM((2, FRAMES, HALF, PX), F32),
        pltpu.VMEM((2, ALL_TILES, 8, 128), F32),
        pltpu.VMEM((2, slots, chips, 8, 128), F32),
        pltpu.VMEM((2, slots, chips, 8, 128), F32),
        pltpu.VMEM((2, ALL_TILES, 8, 128), F32),
        pltpu.VMEM((2, FRAMES, HALF, PX), F32),
        pltpu.VMEM((2, slots, 2, 8, 128), F32),
        pltpu.VMEM((columns_of_space + 1, 8, 128), F32),
        pltpu.SemaphoreType.DMA((2, FRAMES, 2)),
        pltpu.SemaphoreType.DMA((2, FRAMES, 2)),
        pltpu.SemaphoreType.DMA((2, FRAMES)),
        pltpu.SemaphoreType.DMA((2, FRAMES)),
        pltpu.SemaphoreType.DMA((2,)),
        pltpu.SemaphoreType.DMA((2, slots)),
        pltpu.SemaphoreType.DMA((2, slots)),
        pltpu.SemaphoreType.DMA((2, FRAMES)),
        pltpu.SemaphoreType.DMA((2, FRAMES)),
        pltpu.SemaphoreType.DMA((2, FRAMES)),
        pltpu.SemaphoreType.DMA((columns_of_space,)),
        pltpu.SemaphoreType.DMA((columns_of_space,)),
    ]
    return kernel, scratch


def solution(mesh):
    steps, spaces = mesh.shape["step"], mesh.shape["space"]
    cell_count = float(C * FRAMES * PX * spaces)
    kernel, scratch = make_kernel(steps // 2, spaces, cell_count)

    def flat(array):
        cells = array.reshape(C, FRAMES, BLOCKS, 128).transpose(0, 2, 1, 3)
        return cells.reshape(C * BLOCKS * FRAMES, 128)

    def local(guesses, noise, timesteps, conv_first, conv_second, time_weight):
        coef = coefficients(timesteps[0])
        temb = time_embed(timesteps[0, 0], time_weight)[:, None]
        vmem = pl.BlockSpec(memory_space=pltpu.VMEM)
        states, changes = pl.pallas_call(
            kernel,
            out_shape=(
                jax.ShapeDtypeStruct((C * BLOCKS * FRAMES, 128), F32),
                jax.ShapeDtypeStruct((8, 128), F32),
            ),
            in_specs=[pl.BlockSpec(memory_space=pltpu.SMEM)] + [vmem] * 5,
            out_specs=(vmem, vmem),
            scratch_shapes=scratch,
            compiler_params=pltpu.CompilerParams(
                collective_id=0, has_side_effects=True, vmem_limit_bytes=56 * 2**20
            ),
        )(coef, temb, flat(guesses[0]), flat(noise[0]), conv_first, conv_second)
        states = states.reshape(C, BLOCKS, FRAMES, 128).transpose(0, 2, 1, 3)
        return states.reshape(1, C, FRAMES, PX), changes[0, :1]

    in_specs = (
        P("step", None, None, "space"),
        P("step", None, None, "space"),
        P("step", None),
        P(),
        P(),
        P(),
    )
    out_specs = (P("step", None, None, "space"), P("step"))
    return jax.shard_map(local, mesh=mesh, in_specs=in_specs, out_specs=out_specs, check_vma=False)
```

```python
import math

import jax
import jax.numpy as jnp
from jax import lax
from jax.experimental import pallas as pl
from jax.experimental.pallas import tpu as pltpu
from jax.sharding import PartitionSpec as P

C = 64
HID = 256
COLS = 80
FRAMES = 4
BF = jnp.bfloat16
F32 = jnp.float32
MESH = pl.DeviceIdType.MESH

PX = 640
OWN = 256
EXT = OWN + PX + 256
Q0 = 128
NQ = 896
HALF = C // 2
TILES = HALF // 8 * (PX // 128)
BLOCKS = PX // 128
CHUNK = 256


def expm1(value):
    series = 1.0 + value / 11.0
    for n in range(10, 1, -1):
        series = 1.0 + value / n * series
    return jnp.where(jnp.abs(value) < 0.5, value * series, jnp.exp(value) - 1.0)


def plan(timestep):
    scaled = timestep / 1000.0
    return -(0.1 * scaled + 9.95 * scaled * scaled)


def coefficients(before, after):
    log_from = plan(before)
    log_to = plan(after)
    half_gap = 0.5 * (log_to - log_from)
    decay_gain = expm1(half_gap)
    remain_from = -expm1(log_from)
    remain_to = -expm1(log_to)
    ratio_term = -expm1(log_from - log_to)
    noise_gain = -jnp.exp(half_gap) * jnp.sqrt(remain_from) + remain_to * jnp.exp(
        -half_gap
    ) / jnp.sqrt(remain_from)
    spread_gain = jnp.sqrt(remain_to / remain_from * ratio_term)
    return decay_gain, noise_gain, spread_gain


def make_kernel(chips, columns_of_space, cell_count):
    parts = -(-TILES // chips)

    def kernel(
        times, y_hbm, n_hbm, w1_hbm, w2_hbm, tw_hbm, out_hbm, chg_ref,
        ent, ebf, xc, hid, grp, w1r, w2r, twr, w1s, w2s, temb, noise, res,
        st, pb, cs, rx, tx, px, eo, ssq, load_sem, out_sem,
        halo_send, halo_recv, pair_send, pair_recv, cs_send, rx_recv, tx_send, px_recv,
        eo_send, ent_recv, ssq_send, ssq_recv,
    ):
        step = lax.axis_index("step")
        space = lax.axis_index("space")
        chip = step // 2
        core = step - 2 * chip
        other = 1 - core
        partner = 2 * chip + other
        anchor = step == 0
        mine_rows = pl.ds(pl.multiple_of(core * HALF, HALF), HALF)
        other_rows = pl.ds(pl.multiple_of(other * HALF, HALF), HALF)

        loads = [pltpu.make_async_copy(y_hbm.at[:, f, :], ent.at[0, f], load_sem.at[f]) for f in range(FRAMES)]
        loads += [
            pltpu.make_async_copy(n_hbm.at[:, f, :], noise.at[f], load_sem.at[FRAMES + f])
            for f in range(FRAMES)
        ]
        late = [
            pltpu.make_async_copy(tw_hbm, twr, load_sem.at[2 * FRAMES]),
            pltpu.make_async_copy(w1_hbm, w1r, load_sem.at[2 * FRAMES + 1]),
            pltpu.make_async_copy(w2_hbm, w2r, load_sem.at[2 * FRAMES + 2]),
        ]
        for copy in loads[:FRAMES] + late + loads[FRAMES:]:
            copy.start()

        for s in range(2):
            for f in range(FRAMES):
                ebf[s, f, :, 0:OWN] = jnp.zeros((C, OWN), BF)
                ebf[s, f, :, OWN + PX : EXT] = jnp.zeros((C, OWN), BF)

        barrier = pltpu.get_barrier_semaphore()

        @pl.loop(1, chips)
        def _(d):
            target = lax.rem(chip + d, chips)
            pl.semaphore_signal(
                barrier, inc=1, device_id={"step": 2 * target + core}, device_id_type=MESH
            )

        pl.semaphore_signal(barrier, inc=1, device_id={"step": partner}, device_id_type=MESH)
        for d in range(1, columns_of_space):
            pl.semaphore_signal(
                barrier,
                inc=1,
                device_id={"space": lax.rem(space + d, columns_of_space)},
                device_id_type=MESH,
            )

        lane = lax.broadcasted_iota(jnp.int32, (1, EXT), 1)
        column = lax.rem(lane + (4 * COLS - OWN % COLS), COLS)
        not_last = column != COLS - 1
        not_first = column != 0

        def halo_copies(s, f):
            right = pltpu.make_async_remote_copy(
                src_ref=ebf.at[s, f, :, pl.ds(OWN + PX - 256, 256)],
                dst_ref=ebf.at[s, f, :, pl.ds(0, 256)],
                send_sem=halo_send.at[s, f, 0],
                recv_sem=halo_recv.at[s, f, 0],
                device_id={"space": lax.rem(space + 1, columns_of_space)},
                device_id_type=MESH,
            )
            left = pltpu.make_async_remote_copy(
                src_ref=ebf.at[s, f, :, pl.ds(OWN, 256)],
                dst_ref=ebf.at[s, f, :, pl.ds(OWN + PX, 256)],
                send_sem=halo_send.at[s, f, 1],
                recv_sem=halo_recv.at[s, f, 1],
                device_id={"space": lax.rem(space + columns_of_space - 1, columns_of_space)},
                device_id_type=MESH,
            )
            return right, left

        def halo_start(s, f):
            right, left = halo_copies(s, f)

            @pl.when(space < columns_of_space - 1)
            def _():
                right.start()

            @pl.when(space > 0)
            def _():
                left.start()

        def halo_wait(s, f):
            right, left = halo_copies(s, f)

            @pl.when(space > 0)
            def _():
                right.wait_recv()

            @pl.when(space < columns_of_space - 1)
            def _():
                left.wait_recv()

        def halo_done(s, f):
            right, left = halo_copies(s, f)

            @pl.when(space < columns_of_space - 1)
            def _():
                right.wait_send()

            @pl.when(space > 0)
            def _():
                left.wait_send()

        def im2col(s, f):
            halo_wait(s, f)
            whole = ebf[s, f]
            zero = jnp.zeros_like(whole)
            shifted = (jnp.where(not_last, whole, zero), whole, jnp.where(not_first, whole, zero))
            for b in range(3):
                for c in range(3):
                    start = Q0 + COLS * (b - 1) + (c - 1)
                    row = f * 9 * C + (b * 3 + c) * C
                    xc[row : row + C, :] = shifted[c][:, start : start + NQ]

        def conv_one(f):
            low, high = max(f - 1, 0), min(f + 2, FRAMES)
            first = low - f + 1
            weights = w1s[:, 9 * C * first : 9 * C * (first + high - low)]
            for n in range(0, NQ, CHUNK):
                m = min(n + CHUNK, NQ)
                value = jnp.dot(
                    weights, xc[low * 9 * C : high * 9 * C, n:m], preferred_element_type=F32
                )
                value = value + jnp.concatenate([temb[...]] * ((m - n) // 128), axis=1)
                value = value / (1.0 + jnp.exp(-value))
                if n + Q0 < OWN:
                    place = lax.broadcasted_iota(jnp.int32, (1, m - n), 1) + (n + Q0)
                    value = jnp.where((place >= OWN) | (space > 0), value, 0.0)
                if m + Q0 > OWN + PX:
                    place = lax.broadcasted_iota(jnp.int32, (1, m - n), 1) + (n + Q0)
                    value = jnp.where(
                        (place < OWN + PX) | (space < columns_of_space - 1), value, 0.0
                    )
                hid[f * HID : (f + 1) * HID, n:m] = value.astype(BF)

        def conv_two(f):
            low, high = max(f - 1, 0), min(f + 2, FRAMES)
            first = low - f + 1
            weights = w2s[:, HID * first : HID * (first + high - low)]
            for n in range(0, NQ, CHUNK):
                m = min(n + CHUNK, NQ)
                grp[:, n:m] = jnp.dot(
                    weights, hid[low * HID : high * HID, n:m], preferred_element_type=F32
                )
            masks = (not_last[:, Q0 : Q0 + NQ], None, not_first[:, Q0 : Q0 + NQ])
            total = None
            for b in range(3):
                for c in range(3):
                    tap = b * 3 + c
                    value = grp[tap * C : (tap + 1) * C, :]
                    if masks[c] is not None:
                        value = jnp.where(masks[c], value, 0.0)
                    start = OWN - Q0 + COLS * (b - 1) + (c - 1)
                    value = pltpu.roll(value, (NQ - start) % NQ, 1)[:, :PX]
                    total = value if total is None else total + value
            return total

        def pair_copy(s, f):
            return pltpu.make_async_remote_copy(
                src_ref=st.at[s, f, other_rows, :],
                dst_ref=pb.at[s, f],
                send_sem=pair_send.at[s, f],
                recv_sem=pair_recv.at[s, f],
                device_id={"step": partner},
                device_id_type=MESH,
            )

        def drift(s, f):
            latent = ent[s, f]
            value = decay_gain * latent + noise_gain * conv_two(f) + spread_gain * noise[f]
            st[s, f] = value + jnp.where(anchor, latent, 0.0)
            pair_copy(s, f).start()

        def chip_sum(s, f):
            pair_copy(s, f).wait_recv()
            total = st[s, f, mine_rows, :] + pb[s, f]
            for r in range(HALF // 8):
                for b in range(BLOCKS):
                    cs[s, f, r * BLOCKS + b] = total[8 * r : 8 * r + 8, 128 * b : 128 * b + 128]
            for k in range(parts):
                low, high, base = span(f, k)

                @pl.loop(low, high)
                def _(g):
                    owner = g + base
                    owner = jnp.where(owner >= chips, owner - chips, owner)

                    @pl.when(owner != chip)
                    def _():
                        pltpu.make_async_remote_copy(
                            src_ref=cs.at[s, f, g],
                            dst_ref=rx.at[s, f, k, chip],
                            send_sem=cs_send.at[s, f, k],
                            recv_sem=rx_recv.at[s, f, k],
                            device_id={"step": 2 * owner + core},
                            device_id_type=MESH,
                        ).start()

                def keep(g):
                    rx[s, f, k, chip] = cs[s, f, g]

                if_mine(f, k, keep)

        def own(s, f):
            for k in range(parts):

                def work(g):
                    given = rx.at[s, f, k, pl.ds(0, chips - 1)]
                    pltpu.make_async_copy(given, given, rx_recv.at[s, f, k]).wait()
                    running = jnp.zeros((8, 128), F32)
                    for q in range(chips):
                        tx[s, f, k, q] = running
                        running = running + rx[s, f, k, q]

                    @pl.loop(1, chips)
                    def _(d):
                        target = chip + d
                        target = jnp.where(target >= chips, target - chips, target)
                        pltpu.make_async_remote_copy(
                            src_ref=tx.at[s, f, k, target],
                            dst_ref=px.at[s, f, g],
                            send_sem=tx_send.at[s, f, k],
                            recv_sem=px_recv.at[s, f, k],
                            device_id={"step": 2 * target + core},
                            device_id_type=MESH,
                        ).start()

                    px[s, f, g] = tx[s, f, k, chip]

                if_mine(f, k, work)

        def span(f, k):
            low, high = k * chips, min((k + 1) * chips, TILES)
            return low, high, f * TILES % chips - low

        def if_mine(f, k, work, otherwise=None):
            low, high, base = span(f, k)
            g = chip - base
            g = jnp.where(g < low, g + chips, g)
            if high - low == chips:
                work(g)
            else:
                pl.when(g < high)(lambda: work(g))
                if otherwise is not None:
                    pl.when(g >= high)(lambda: otherwise(g))

        def tiles_wait(ref, sem, s, f):
            for k in range(parts):
                low, high, _ = span(f, k)

                def wait(count):
                    tiles = ref.at[s, f, pl.ds(0, count)]
                    return lambda g: pltpu.make_async_copy(tiles, tiles, sem.at[s, f, k]).wait()

                if_mine(f, k, wait(high - low - 1), wait(high - low))

        def scan_done(s, f):
            tiles_wait(cs, cs_send, s, f)
            for k in range(parts):

                def wait(g):
                    sent = tx.at[s, f, k, pl.ds(0, chips - 1)]
                    pltpu.make_async_copy(sent, sent, tx_send.at[s, f, k]).wait()

                if_mine(f, k, wait)

        def enter_copy(s, f):
            return pltpu.make_async_remote_copy(
                src_ref=eo.at[s, f],
                dst_ref=ent.at[s + 1, f, mine_rows, :],
                send_sem=eo_send.at[s, f],
                recv_sem=ent_recv.at[s, f],
                device_id={"step": partner},
                device_id_type=MESH,
            )

        def enter(s, f):
            tiles_wait(px, px_recv, s, f)
            before = jnp.concatenate(
                [
                    jnp.concatenate(
                        [px[s, f, r * BLOCKS + b] for b in range(BLOCKS)], axis=1
                    )
                    for r in range(HALF // 8)
                ],
                axis=0,
            )
            first = jnp.where(core == 0, st[s, f, mine_rows, :], pb[s, f])
            after = before + first
            eo[s, f] = jnp.where(core == 0, after, before)
            enter_copy(s, f).start()
            ent[s + 1, f, mine_rows, :] = jnp.where(core == 0, before, after)

        def entered(s, f):
            pltpu.make_async_copy(
                ent.at[s + 1, f, other_rows, :], ent.at[s + 1, f, other_rows, :], ent_recv.at[s, f]
            ).wait()

            @pl.when(anchor)
            def _():
                ent[s + 1, f] = ent[0, f]

        def latent_out(s, f):
            ebf[s, f, :, OWN : OWN + PX] = ent[s, f].astype(BF)
            halo_start(s, f)

        before = jnp.full((8, 128), times[0, 0], jnp.int32).astype(F32)
        after = jnp.full((8, 128), times[0, 1], jnp.int32).astype(F32)
        decay_gain, noise_gain, spread_gain = [
            gain[0:1, 0:1] for gain in coefficients(before, after)
        ]
        index = lax.broadcasted_iota(jnp.int32, (C, 128), 0)
        sine = index < C // 2
        place = jnp.where(sine, index, index - C // 2).astype(F32)
        frequency = jnp.exp(-math.log(10000.0) * place / (C // 2))
        angles = before[0:1, :] * frequency
        features = jnp.where(sine, jnp.sin(angles), jnp.cos(angles))
        for copy in loads[:FRAMES]:
            copy.wait()
        for f in range(FRAMES):
            ebf[0, f, :, OWN : OWN + PX] = ent[0, f].astype(BF)
        late[0].wait()
        for n in range(0, HID, 128):
            row = jnp.sum(twr[:, n : n + 128] * features, axis=0, keepdims=True)
            temb[n : n + 128, :] = jnp.broadcast_to(row, (128, 128)).T
        late[1].wait()
        for n in range(0, 27 * C, 128):
            m = min(n + 128, 27 * C)
            w1s[:, n:m] = w1r[n:m, :].T
        late[2].wait()
        for a in range(3):
            for tap in range(9):
                w2s[tap * C : (tap + 1) * C, a * HID : (a + 1) * HID] = w2r[
                    a, :, tap * HID : (tap + 1) * HID
                ]
        for copy in loads[FRAMES:]:
            copy.wait()

        pl.semaphore_wait(barrier, chips + columns_of_space - 1)
        for f in range(FRAMES):
            halo_start(0, f)

        def out_copy(f):
            return pltpu.make_async_copy(res.at[f], out_hbm.at[:, f, :], out_sem.at[f])

        for s in range(2):
            im2col(s, 0)
            im2col(s, 1)
            conv_one(0)
            im2col(s, 2)
            conv_one(1)
            drift(s, 0)
            im2col(s, 3)
            conv_one(2)
            chip_sum(s, 0)
            drift(s, 1)
            conv_one(3)
            chip_sum(s, 1)
            drift(s, 2)
            chip_sum(s, 2)
            drift(s, 3)
            chip_sum(s, 3)
            for f in range(FRAMES):
                own(s, f)
            square = None
            enter(s, 0)
            for f in range(FRAMES):
                if f + 1 < FRAMES:
                    enter(s, f + 1)
                entered(s, f)
                if s == 0:
                    latent_out(1, f)
                else:
                    keep = jnp.where(anchor, 0.0, 1.0)
                    reached = keep * ent[2, f] + st[1, f]
                    change = reached - (keep * ent[1, f] + st[0, f])
                    change = change * change
                    for r in range(C // 8):
                        for b in range(BLOCKS):
                            part = change[8 * r : 8 * r + 8, 128 * b : 128 * b + 128]
                            square = part if square is None else square + part
                    res[f] = reached
                    out_copy(f).start()
            if s == 1:
                ssq[0] = square

        def ssq_copy(d):
            return pltpu.make_async_remote_copy(
                src_ref=ssq.at[0],
                dst_ref=ssq.at[columns_of_space + 1 - d],
                send_sem=ssq_send.at[d - 1],
                recv_sem=ssq_recv.at[columns_of_space - 1 - d],
                device_id={"space": lax.rem(space + d, columns_of_space)},
                device_id_type=MESH,
            )

        for d in range(1, columns_of_space):
            ssq_copy(d).start()

        for s in range(2):
            for f in range(FRAMES):
                halo_done(s, f)
                pair_copy(s, f).wait_send()
                enter_copy(s, f).wait_send()
                scan_done(s, f)
        for f in range(FRAMES):
            out_copy(f).wait()

        for d in range(1, columns_of_space):
            ssq_copy(d).wait_send()
        for d in range(1, columns_of_space):
            ssq_copy(columns_of_space - d).wait_recv()
        total = None
        for x in range(columns_of_space):
            part = None
            for d in range(columns_of_space):
                place = 0 if d == 0 else d + 1
                term = jnp.where(lax.rem(space + d, columns_of_space) == x, ssq[place], 0.0)
                part = term if part is None else part + term
            total = part if total is None else total + part
        mean = jnp.full((8, 128), jnp.sum(total), F32) / cell_count
        chg_ref[0] = jnp.max(jnp.sqrt(mean))

    scratch = [
        pltpu.VMEM((3, FRAMES, C, PX), F32),
        pltpu.VMEM((2, FRAMES, C, EXT), BF),
        pltpu.VMEM((FRAMES * 9 * C, NQ), BF),
        pltpu.VMEM((FRAMES * HID, NQ), BF),
        pltpu.VMEM((9 * C, NQ), F32),
        pltpu.VMEM((27 * C, HID), BF),
        pltpu.VMEM((3, C, 9 * HID), BF),
        pltpu.VMEM((C, HID), F32),
        pltpu.VMEM((HID, 27 * C), BF),
        pltpu.VMEM((9 * C, 3 * HID), BF),
        pltpu.VMEM((HID, 128), F32),
        pltpu.VMEM((FRAMES, C, PX), F32),
        pltpu.VMEM((FRAMES, C, PX), F32),
        pltpu.VMEM((2, FRAMES, C, PX), F32),
        pltpu.VMEM((2, FRAMES, HALF, PX), F32),
        pltpu.VMEM((2, FRAMES, TILES, 8, 128), F32),
        pltpu.VMEM((2, FRAMES, parts, chips, 8, 128), F32),
        pltpu.VMEM((2, FRAMES, parts, chips, 8, 128), F32),
        pltpu.VMEM((2, FRAMES, TILES, 8, 128), F32),
        pltpu.VMEM((2, FRAMES, HALF, PX), F32),
        pltpu.VMEM((columns_of_space + 1, 8, 128), F32),
        pltpu.SemaphoreType.DMA((2 * FRAMES + 3,)),
        pltpu.SemaphoreType.DMA((FRAMES,)),
        pltpu.SemaphoreType.DMA((2, FRAMES, 2)),
        pltpu.SemaphoreType.DMA((2, FRAMES, 2)),
        pltpu.SemaphoreType.DMA((2, FRAMES)),
        pltpu.SemaphoreType.DMA((2, FRAMES)),
        pltpu.SemaphoreType.DMA((2, FRAMES, parts)),
        pltpu.SemaphoreType.DMA((2, FRAMES, parts)),
        pltpu.SemaphoreType.DMA((2, FRAMES, parts)),
        pltpu.SemaphoreType.DMA((2, FRAMES, parts)),
        pltpu.SemaphoreType.DMA((2, FRAMES)),
        pltpu.SemaphoreType.DMA((2, FRAMES)),
        pltpu.SemaphoreType.DMA((columns_of_space,)),
        pltpu.SemaphoreType.DMA((columns_of_space,)),
    ]
    return kernel, scratch


def solution(mesh):
    steps, spaces = mesh.shape["step"], mesh.shape["space"]
    cell_count = float(C * FRAMES * PX * spaces)
    kernel, scratch = make_kernel(steps // 2, spaces, cell_count)

    def local(guesses, noise, timesteps, conv_first, conv_second, time_weight):
        anywhere = pl.BlockSpec(memory_space=pl.ANY)
        scalars = pl.BlockSpec(memory_space=pltpu.SMEM)
        first = conv_first.transpose(0, 2, 1).reshape(27 * C, HID)
        states, changes = pl.pallas_call(
            kernel,
            out_shape=(
                jax.ShapeDtypeStruct((C, FRAMES, PX), F32),
                jax.ShapeDtypeStruct((1,), F32),
            ),
            in_specs=[scalars] + [anywhere] * 5,
            out_specs=(anywhere, scalars),
            scratch_shapes=scratch,
            compiler_params=pltpu.CompilerParams(
                collective_id=0, has_side_effects=True, vmem_limit_bytes=56 * 2**20
            ),
        )(timesteps, guesses[0], noise[0], first, conv_second, time_weight)
        return states[None], changes

    in_specs = (
        P("step", None, None, "space"),
        P("step", None, None, "space"),
        P("step", None),
        P(),
        P(),
        P(),
    )
    out_specs = (P("step", None, None, "space"), P("step"))
    return jax.shard_map(local, mesh=mesh, in_specs=in_specs, out_specs=out_specs, check_vma=False)
```

```python
import math

import jax
import jax.numpy as jnp
from jax import lax
from jax.experimental import pallas as pl
from jax.experimental.pallas import tpu as pltpu
from jax.sharding import PartitionSpec as P

C = 64
HID = 256
COLS = 80
FRAMES = 4
BF = jnp.bfloat16
F32 = jnp.float32
MESH = pl.DeviceIdType.MESH

PX = 640
OWN = 256
EXT = OWN + PX + 256
Q0 = 128
NQ = 896
HALF = C // 2
TILES = HALF // 8 * (PX // 128)
BLOCKS = PX // 128
CHUNK = 256


def expm1(value):
    series = 1.0 + value / 11.0
    for n in range(10, 1, -1):
        series = 1.0 + value / n * series
    return jnp.where(jnp.abs(value) < 0.5, value * series, jnp.exp(value) - 1.0)


def plan(timestep):
    scaled = timestep / 1000.0
    return -(0.1 * scaled + 9.95 * scaled * scaled)


def coefficients(before, after):
    log_from = plan(before)
    log_to = plan(after)
    half_gap = 0.5 * (log_to - log_from)
    decay_gain = expm1(half_gap)
    remain_from = -expm1(log_from)
    remain_to = -expm1(log_to)
    ratio_term = -expm1(log_from - log_to)
    noise_gain = -jnp.exp(half_gap) * jnp.sqrt(remain_from) + remain_to * jnp.exp(
        -half_gap
    ) / jnp.sqrt(remain_from)
    spread_gain = jnp.sqrt(remain_to / remain_from * ratio_term)
    return decay_gain, noise_gain, spread_gain


def make_kernel(chips, columns_of_space, cell_count):
    parts = -(-TILES // chips)
    wide = min(4, chips)
    deep = chips // wide
    far = max(1, chips // 2 - 2)

    def kernel(
        times, y_hbm, n_hbm, w1_hbm, w2_hbm, tw_hbm, out_hbm, chg_ref,
        ent, ebf, xc, hid, grp, w1r, w2r, twr, w1s, w2s, temb, noise, res,
        st, pb, cs, rx, tx, px, eo, ssq, load_sem, out_sem, near,
        halo_send, halo_recv, pair_send, pair_recv, cs_send, rx_recv, tx_send, px_recv,
        eo_send, ent_recv, ssq_send, ssq_recv,
    ):
        step = lax.axis_index("step")
        space = lax.axis_index("space")
        chip = step // 2
        core = step - 2 * chip
        chip_z = chip // wide
        chip_y = chip - chip_z * wide
        other = 1 - core
        partner = 2 * chip + other
        anchor = step == 0
        mine_rows = pl.ds(pl.multiple_of(core * HALF, HALF), HALF)
        other_rows = pl.ds(pl.multiple_of(other * HALF, HALF), HALF)

        loads = [pltpu.make_async_copy(y_hbm.at[:, f, :], ent.at[0, f], load_sem.at[f]) for f in range(FRAMES)]
        loads += [
            pltpu.make_async_copy(n_hbm.at[:, f, :], noise.at[f], load_sem.at[FRAMES + f])
            for f in range(FRAMES)
        ]
        late = [
            pltpu.make_async_copy(tw_hbm, twr, load_sem.at[2 * FRAMES]),
            pltpu.make_async_copy(w1_hbm, w1r, load_sem.at[2 * FRAMES + 1]),
            pltpu.make_async_copy(w2_hbm, w2r, load_sem.at[2 * FRAMES + 2]),
        ]
        for copy in loads[:FRAMES] + late + loads[FRAMES:]:
            copy.start()

        for s in range(2):
            for f in range(FRAMES):
                ebf[s, f, :, 0:OWN] = jnp.zeros((C, OWN), BF)
                ebf[s, f, :, OWN + PX : EXT] = jnp.zeros((C, OWN), BF)

        barrier = pltpu.get_barrier_semaphore()

        def signal(sem, **place):
            pl.semaphore_signal(sem, inc=1, device_id=place, device_id_type=MESH)

        def along_z(d):
            return 2 * (lax.rem(chip_z + d + deep, deep) * wide + chip_y) + core

        def along_y(d):
            return 2 * (chip_z * wide + lax.rem(chip_y + d, wide)) + core

        for d in range(1, columns_of_space):
            signal(barrier, space=lax.rem(space + d, columns_of_space))
        signal(barrier, step=partner)
        for d in range(1, wide):
            signal(barrier, step=along_y(d))
        close = columns_of_space + wide - 1
        if deep > 1:
            signal(barrier, step=along_z(1))
            signal(barrier, step=along_z(-1))
            close += 2

        def greet(n):
            if n < 2 and deep > 1:
                signal(near.at[n], step=along_z(n + 1))
                signal(near.at[n], step=along_z(-n - 1))
            if n == 2:
                for d in range(1, wide):
                    signal(near.at[n], step=along_y(d))

        def greeted(n):
            if n < 2 and deep > 1:
                pl.semaphore_wait(near.at[n], 2)
            if n == 2:
                pl.semaphore_wait(near.at[n], wide - 1)

        lane = lax.broadcasted_iota(jnp.int32, (1, EXT), 1)
        column = lax.rem(lane + (4 * COLS - OWN % COLS), COLS)
        not_last = column != COLS - 1
        not_first = column != 0

        def halo_copies(s, f):
            right = pltpu.make_async_remote_copy(
                src_ref=ebf.at[s, f, :, pl.ds(OWN + PX - 256, 256)],
                dst_ref=ebf.at[s, f, :, pl.ds(0, 256)],
                send_sem=halo_send.at[s, f, 0],
                recv_sem=halo_recv.at[s, f, 0],
                device_id={"space": lax.rem(space + 1, columns_of_space)},
                device_id_type=MESH,
            )
            left = pltpu.make_async_remote_copy(
                src_ref=ebf.at[s, f, :, pl.ds(OWN, 256)],
                dst_ref=ebf.at[s, f, :, pl.ds(OWN + PX, 256)],
                send_sem=halo_send.at[s, f, 1],
                recv_sem=halo_recv.at[s, f, 1],
                device_id={"space": lax.rem(space + columns_of_space - 1, columns_of_space)},
                device_id_type=MESH,
            )
            return right, left

        def halo_start(s, f):
            right, left = halo_copies(s, f)

            @pl.when(space < columns_of_space - 1)
            def _():
                right.start()

            @pl.when(space > 0)
            def _():
                left.start()

        def halo_wait(s, f):
            right, left = halo_copies(s, f)

            @pl.when(space > 0)
            def _():
                right.wait_recv()

            @pl.when(space < columns_of_space - 1)
            def _():
                left.wait_recv()

        def halo_done(s, f):
            right, left = halo_copies(s, f)

            @pl.when(space < columns_of_space - 1)
            def _():
                right.wait_send()

            @pl.when(space > 0)
            def _():
                left.wait_send()

        def im2col(s, f):
            halo_wait(s, f)
            whole = ebf[s, f]
            zero = jnp.zeros_like(whole)
            shifted = (jnp.where(not_last, whole, zero), whole, jnp.where(not_first, whole, zero))
            for b in range(3):
                for c in range(3):
                    start = Q0 + COLS * (b - 1) + (c - 1)
                    row = f * 9 * C + (b * 3 + c) * C
                    xc[row : row + C, :] = shifted[c][:, start : start + NQ]

        def conv_one(f):
            low, high = max(f - 1, 0), min(f + 2, FRAMES)
            first = low - f + 1
            weights = w1s[:, 9 * C * first : 9 * C * (first + high - low)]
            for n in range(0, NQ, CHUNK):
                m = min(n + CHUNK, NQ)
                value = jnp.dot(
                    weights, xc[low * 9 * C : high * 9 * C, n:m], preferred_element_type=F32
                )
                value = value + jnp.concatenate([temb[...]] * ((m - n) // 128), axis=1)
                value = value / (1.0 + jnp.exp(-value))
                if n + Q0 < OWN:
                    place = lax.broadcasted_iota(jnp.int32, (1, m - n), 1) + (n + Q0)
                    value = jnp.where((place >= OWN) | (space > 0), value, 0.0)
                if m + Q0 > OWN + PX:
                    place = lax.broadcasted_iota(jnp.int32, (1, m - n), 1) + (n + Q0)
                    value = jnp.where(
                        (place < OWN + PX) | (space < columns_of_space - 1), value, 0.0
                    )
                hid[f * HID : (f + 1) * HID, n:m] = value.astype(BF)

        def conv_two(f):
            low, high = max(f - 1, 0), min(f + 2, FRAMES)
            first = low - f + 1
            weights = w2s[:, HID * first : HID * (first + high - low)]
            for n in range(0, NQ, CHUNK):
                m = min(n + CHUNK, NQ)
                grp[f % 2, :, n:m] = jnp.dot(
                    weights, hid[low * HID : high * HID, n:m], preferred_element_type=F32
                )

        def combine(f):
            masks = (not_last[:, Q0 : Q0 + NQ], None, not_first[:, Q0 : Q0 + NQ])
            total = None
            for b in range(3):
                for c in range(3):
                    tap = b * 3 + c
                    value = grp[f % 2, tap * C : (tap + 1) * C, :]
                    if masks[c] is not None:
                        value = jnp.where(masks[c], value, 0.0)
                    start = OWN - Q0 + COLS * (b - 1) + (c - 1)
                    value = pltpu.roll(value, (NQ - start) % NQ, 1)[:, :PX]
                    total = value if total is None else total + value
            return total

        def pair_copy(s, f):
            return pltpu.make_async_remote_copy(
                src_ref=st.at[s, f, other_rows, :],
                dst_ref=pb.at[s, f],
                send_sem=pair_send.at[s, f],
                recv_sem=pair_recv.at[s, f],
                device_id={"step": partner},
                device_id_type=MESH,
            )

        def drift(s, f):
            latent = ent[s, f]
            value = decay_gain * latent + noise_gain * combine(f) + spread_gain * noise[f]
            st[s, f] = value + jnp.where(anchor, latent, 0.0)
            pair_copy(s, f).start()

        def chip_sum(s, f):
            pair_copy(s, f).wait_recv()
            total = st[s, f, mine_rows, :] + pb[s, f]
            for r in range(HALF // 8):
                for b in range(BLOCKS):
                    cs[s, f, r * BLOCKS + b] = total[8 * r : 8 * r + 8, 128 * b : 128 * b + 128]
            for k in range(parts):
                low, high, base = span(f, k)

                for g in range(low, high):
                    owner = (g + base) % chips
                    own_tile = chip == owner
                    pltpu.make_async_remote_copy(
                        src_ref=cs.at[s, f, g],
                        dst_ref=rx.at[s, f, k, jnp.where(own_tile, chips, chip)],
                        send_sem=cs_send.at[s, f, k],
                        recv_sem=rx_recv.at[s, f, k],
                        device_id={"step": jnp.where(own_tile, partner, 2 * owner + core)},
                        device_id_type=MESH,
                    ).start()

                def keep(g):
                    rx[s, f, k, chip] = cs[s, f, g]

                if_mine(f, k, keep)

        def own(s, f):
            for k in range(parts):

                def work(g):
                    given = rx.at[s, f, k, pl.ds(0, chips)]
                    pltpu.make_async_copy(given, given, rx_recv.at[s, f, k]).wait()
                    running = jnp.zeros((8, 128), F32)
                    for q in range(chips):
                        tx[s, f, k, q] = running
                        running = running + rx[s, f, k, q]

                    @pl.loop(far, far + chips - 1)
                    def _(d):
                        target = chip + jnp.where(d >= chips, d - chips + 1, d)
                        target = jnp.where(target >= chips, target - chips, target)
                        pltpu.make_async_remote_copy(
                            src_ref=tx.at[s, f, k, target],
                            dst_ref=px.at[s, f, g],
                            send_sem=tx_send.at[s, f, k],
                            recv_sem=px_recv.at[s, f, k],
                            device_id={"step": 2 * target + core},
                            device_id_type=MESH,
                        ).start()

                    px[s, f, g] = tx[s, f, k, chip]

                if_mine(f, k, work)

        def span(f, k):
            low, high = k * chips, min((k + 1) * chips, TILES)
            return low, high, f * TILES % chips - low

        def if_mine(f, k, work, otherwise=None):
            low, high, base = span(f, k)
            g = chip - base
            g = jnp.where(g < low, g + chips, g)
            if high - low == chips:
                work(g)
            else:
                pl.when(g < high)(lambda: work(g))
                if otherwise is not None:
                    pl.when(g >= high)(lambda: otherwise(g))

        def tiles_wait(ref, sem, s, f):
            for k in range(parts):
                low, high, _ = span(f, k)

                def wait(count):
                    tiles = ref.at[s, f, pl.ds(0, count)]
                    return lambda g: pltpu.make_async_copy(tiles, tiles, sem.at[s, f, k]).wait()

                if_mine(f, k, wait(high - low - 1), wait(high - low))

        def scan_done(s, f):
            for k in range(parts):
                low, high, _ = span(f, k)
                tiles = cs.at[s, f, pl.ds(low, high - low)]
                pltpu.make_async_copy(tiles, tiles, cs_send.at[s, f, k]).wait()

                def wait(g):
                    sent = tx.at[s, f, k, pl.ds(0, chips - 1)]
                    pltpu.make_async_copy(sent, sent, tx_send.at[s, f, k]).wait()

                if_mine(f, k, wait)

        def enter_copy(s, f):
            return pltpu.make_async_remote_copy(
                src_ref=eo.at[s, f],
                dst_ref=ent.at[s + 1, f, mine_rows, :],
                send_sem=eo_send.at[s, f],
                recv_sem=ent_recv.at[s, f],
                device_id={"step": partner},
                device_id_type=MESH,
            )

        def enter(s, f):
            tiles_wait(px, px_recv, s, f)
            before = jnp.concatenate(
                [
                    jnp.concatenate(
                        [px[s, f, r * BLOCKS + b] for b in range(BLOCKS)], axis=1
                    )
                    for r in range(HALF // 8)
                ],
                axis=0,
            )
            first = jnp.where(core == 0, st[s, f, mine_rows, :], pb[s, f])
            after = before + first
            eo[s, f] = jnp.where(core == 0, after, before)
            enter_copy(s, f).start()
            ent[s + 1, f, mine_rows, :] = jnp.where(core == 0, before, after)

        def entered(s, f):
            pltpu.make_async_copy(
                ent.at[s + 1, f, other_rows, :], ent.at[s + 1, f, other_rows, :], ent_recv.at[s, f]
            ).wait()

            @pl.when(anchor)
            def _():
                ent[s + 1, f] = ent[0, f]

        def latent_out(s, f):
            ebf[s, f, :, OWN : OWN + PX] = ent[s, f].astype(BF)
            halo_start(s, f)

        for copy in loads[:FRAMES]:
            copy.wait()
        for f in range(FRAMES):
            ebf[0, f, :, OWN : OWN + PX] = ent[0, f].astype(BF)

        pl.semaphore_wait(barrier, close)
        greet(0)
        for f in range(FRAMES):
            halo_start(0, f)

        before = jnp.full((8, 128), times[0, 0], jnp.int32).astype(F32)
        after = jnp.full((8, 128), times[0, 1], jnp.int32).astype(F32)
        decay_gain, noise_gain, spread_gain = [
            gain[0:1, 0:1] for gain in coefficients(before, after)
        ]
        index = lax.broadcasted_iota(jnp.int32, (C, 128), 0)
        sine = index < C // 2
        place = jnp.where(sine, index, index - C // 2).astype(F32)
        frequency = jnp.exp(-math.log(10000.0) * place / (C // 2))
        angles = before[0:1, :] * frequency
        features = jnp.where(sine, jnp.sin(angles), jnp.cos(angles))
        late[0].wait()
        for n in range(0, HID, 128):
            row = jnp.sum(twr[:, n : n + 128] * features, axis=0, keepdims=True)
            temb[n : n + 128, :] = jnp.broadcast_to(row, (128, 128)).T
        late[1].wait()
        for n in range(0, 27 * C, 128):
            m = min(n + 128, 27 * C)
            w1s[:, n:m] = w1r[n:m, :].T
        late[2].wait()
        for a in range(3):
            for tap in range(9):
                w2s[tap * C : (tap + 1) * C, a * HID : (a + 1) * HID] = w2r[
                    a, :, tap * HID : (tap + 1) * HID
                ]
        for copy in loads[FRAMES:]:
            copy.wait()

        def out_copy(f):
            return pltpu.make_async_copy(res.at[f], out_hbm.at[:, f, :], out_sem.at[f])

        for s in range(2):
            im2col(s, 0)
            im2col(s, 1)
            if s == 0:
                greeted(0)
                greet(1)
            conv_one(0)
            im2col(s, 2)
            if s == 0:
                greeted(1)
                greet(2)
            conv_one(1)
            conv_two(0)
            drift(s, 0)
            im2col(s, 3)
            conv_one(2)
            if s == 0:
                greeted(2)
            chip_sum(s, 0)
            conv_two(1)
            conv_one(3)
            drift(s, 1)
            conv_two(2)
            conv_two(3)
            drift(s, 2)
            chip_sum(s, 1)
            drift(s, 3)
            chip_sum(s, 2)
            chip_sum(s, 3)
            for f in range(FRAMES):
                own(s, f)
            square = None
            enter(s, 0)
            for f in range(FRAMES):
                if f + 1 < FRAMES:
                    enter(s, f + 1)
                entered(s, f)
                if s == 0:
                    latent_out(1, f)
                else:
                    keep = jnp.where(anchor, 0.0, 1.0)
                    reached = keep * ent[2, f] + st[1, f]
                    change = reached - (keep * ent[1, f] + st[0, f])
                    change = change * change
                    for r in range(C // 8):
                        for b in range(BLOCKS):
                            part = change[8 * r : 8 * r + 8, 128 * b : 128 * b + 128]
                            square = part if square is None else square + part
                    res[f] = reached
                    out_copy(f).start()
            if s == 1:
                ssq[0] = square

        def ssq_copy(d):
            return pltpu.make_async_remote_copy(
                src_ref=ssq.at[0],
                dst_ref=ssq.at[columns_of_space + 1 - d],
                send_sem=ssq_send.at[d - 1],
                recv_sem=ssq_recv.at[columns_of_space - 1 - d],
                device_id={"space": lax.rem(space + d, columns_of_space)},
                device_id_type=MESH,
            )

        for d in range(1, columns_of_space):
            ssq_copy(d).start()

        for s in range(2):
            for f in range(FRAMES):
                halo_done(s, f)
                pair_copy(s, f).wait_send()
                enter_copy(s, f).wait_send()
                scan_done(s, f)
        for f in range(FRAMES):
            out_copy(f).wait()

        for d in range(1, columns_of_space):
            ssq_copy(d).wait_send()
        for d in range(1, columns_of_space):
            ssq_copy(columns_of_space - d).wait_recv()
        total = None
        for x in range(columns_of_space):
            part = None
            for d in range(columns_of_space):
                place = 0 if d == 0 else d + 1
                term = jnp.where(lax.rem(space + d, columns_of_space) == x, ssq[place], 0.0)
                part = term if part is None else part + term
            total = part if total is None else total + part
        mean = jnp.full((8, 128), jnp.sum(total), F32) / cell_count
        chg_ref[0] = jnp.max(jnp.sqrt(mean))

    scratch = [
        pltpu.VMEM((3, FRAMES, C, PX), F32),
        pltpu.VMEM((2, FRAMES, C, EXT), BF),
        pltpu.VMEM((FRAMES * 9 * C, NQ), BF),
        pltpu.VMEM((FRAMES * HID, NQ), BF),
        pltpu.VMEM((2, 9 * C, NQ), F32),
        pltpu.VMEM((27 * C, HID), BF),
        pltpu.VMEM((3, C, 9 * HID), BF),
        pltpu.VMEM((C, HID), F32),
        pltpu.VMEM((HID, 27 * C), BF),
        pltpu.VMEM((9 * C, 3 * HID), BF),
        pltpu.VMEM((HID, 128), F32),
        pltpu.VMEM((FRAMES, C, PX), F32),
        pltpu.VMEM((FRAMES, C, PX), F32),
        pltpu.VMEM((2, FRAMES, C, PX), F32),
        pltpu.VMEM((2, FRAMES, HALF, PX), F32),
        pltpu.VMEM((2, FRAMES, TILES, 8, 128), F32),
        pltpu.VMEM((2, FRAMES, parts, chips + 1, 8, 128), F32),
        pltpu.VMEM((2, FRAMES, parts, chips, 8, 128), F32),
        pltpu.VMEM((2, FRAMES, TILES, 8, 128), F32),
        pltpu.VMEM((2, FRAMES, HALF, PX), F32),
        pltpu.VMEM((columns_of_space + 1, 8, 128), F32),
        pltpu.SemaphoreType.DMA((2 * FRAMES + 3,)),
        pltpu.SemaphoreType.DMA((FRAMES,)),
        pltpu.SemaphoreType.REGULAR((3,)),
        pltpu.SemaphoreType.DMA((2, FRAMES, 2)),
        pltpu.SemaphoreType.DMA((2, FRAMES, 2)),
        pltpu.SemaphoreType.DMA((2, FRAMES)),
        pltpu.SemaphoreType.DMA((2, FRAMES)),
        pltpu.SemaphoreType.DMA((2, FRAMES, parts)),
        pltpu.SemaphoreType.DMA((2, FRAMES, parts)),
        pltpu.SemaphoreType.DMA((2, FRAMES, parts)),
        pltpu.SemaphoreType.DMA((2, FRAMES, parts)),
        pltpu.SemaphoreType.DMA((2, FRAMES)),
        pltpu.SemaphoreType.DMA((2, FRAMES)),
        pltpu.SemaphoreType.DMA((columns_of_space,)),
        pltpu.SemaphoreType.DMA((columns_of_space,)),
    ]
    return kernel, scratch


def solution(mesh):
    steps, spaces = mesh.shape["step"], mesh.shape["space"]
    cell_count = float(C * FRAMES * PX * spaces)
    kernel, scratch = make_kernel(steps // 2, spaces, cell_count)

    def local(guesses, noise, timesteps, conv_first, conv_second, time_weight):
        anywhere = pl.BlockSpec(memory_space=pl.ANY)
        scalars = pl.BlockSpec(memory_space=pltpu.SMEM)
        first = conv_first.transpose(0, 2, 1).reshape(27 * C, HID)
        states, changes = pl.pallas_call(
            kernel,
            out_shape=(
                jax.ShapeDtypeStruct((C, FRAMES, PX), F32),
                jax.ShapeDtypeStruct((1,), F32),
            ),
            in_specs=[scalars] + [anywhere] * 5,
            out_specs=(anywhere, scalars),
            scratch_shapes=scratch,
            compiler_params=pltpu.CompilerParams(
                collective_id=0, has_side_effects=True, vmem_limit_bytes=56 * 2**20
            ),
        )(timesteps, guesses[0], noise[0], first, conv_second, time_weight)
        return states[None], changes

    in_specs = (
        P("step", None, None, "space"),
        P("step", None, None, "space"),
        P("step", None),
        P(),
        P(),
        P(),
    )
    out_specs = (P("step", None, None, "space"), P("step"))
    return jax.shard_map(local, mesh=mesh, in_specs=in_specs, out_specs=out_specs, check_vma=False)
```

```python
import math

import jax
import jax.numpy as jnp
from jax import lax
from jax.experimental import pallas as pl
from jax.experimental.pallas import tpu as pltpu
from jax.sharding import PartitionSpec as P

C = 64
HID = 256
COLS = 80
FRAMES = 4
BF = jnp.bfloat16
F32 = jnp.float32
MESH = pl.DeviceIdType.MESH

PX = 640
OWN = 256
EXT = OWN + PX + 256
Q0 = 128
NQ = 896
HALF = C // 2
TILES = HALF // 8 * (PX // 128)
BLOCKS = PX // 128
CHUNK = 256


def expm1(value):
    series = 1.0 + value / 11.0
    for n in range(10, 1, -1):
        series = 1.0 + value / n * series
    return jnp.where(jnp.abs(value) < 0.5, value * series, jnp.exp(value) - 1.0)


def plan(timestep):
    scaled = timestep / 1000.0
    return -(0.1 * scaled + 9.95 * scaled * scaled)


def coefficients(before, after):
    log_from = plan(before)
    log_to = plan(after)
    half_gap = 0.5 * (log_to - log_from)
    decay_gain = expm1(half_gap)
    remain_from = -expm1(log_from)
    remain_to = -expm1(log_to)
    ratio_term = -expm1(log_from - log_to)
    noise_gain = -jnp.exp(half_gap) * jnp.sqrt(remain_from) + remain_to * jnp.exp(
        -half_gap
    ) / jnp.sqrt(remain_from)
    spread_gain = jnp.sqrt(remain_to / remain_from * ratio_term)
    return decay_gain, noise_gain, spread_gain


def make_kernel(chips, columns_of_space, cell_count):
    parts = -(-TILES // chips)
    wide = min(4, chips)
    deep = chips // wide
    far = max(1, chips // 2 - 2)

    def kernel(
        times, y_hbm, n_hbm, w1_hbm, w2_hbm, tw_hbm, out_hbm, chg_ref,
        ent, ebf, xc, hid, grp, w1r, w2r, twr, w1s, w2s, temb, noise, res,
        st, pb, cs, rx, tx, px, eo, eob, ssq, red, load_sem, out_sem, near,
        halo_send, halo_recv, pair_send, pair_recv, cs_send, rx_recv, tx_send, px_recv,
        eo_send, ent_recv, half_send, red_send, red_recv,
    ):
        step = lax.axis_index("step")
        space = lax.axis_index("space")
        chip = step // 2
        core = step - 2 * chip
        chip_z = chip // wide
        chip_y = chip - chip_z * wide
        other = 1 - core
        partner = 2 * chip + other
        anchor = step == 0
        mine_rows = pl.ds(pl.multiple_of(core * HALF, HALF), HALF)
        other_rows = pl.ds(pl.multiple_of(other * HALF, HALF), HALF)

        loads = [pltpu.make_async_copy(y_hbm.at[:, f, :], ent.at[0, f], load_sem.at[f]) for f in range(FRAMES)]
        loads += [
            pltpu.make_async_copy(n_hbm.at[:, f, :], noise.at[f], load_sem.at[FRAMES + f])
            for f in range(FRAMES)
        ]
        late = [
            pltpu.make_async_copy(tw_hbm, twr, load_sem.at[2 * FRAMES]),
            pltpu.make_async_copy(w1_hbm, w1r, load_sem.at[2 * FRAMES + 1]),
            pltpu.make_async_copy(w2_hbm, w2r, load_sem.at[2 * FRAMES + 2]),
        ]
        for copy in loads[:FRAMES] + late + loads[FRAMES:]:
            copy.start()

        for s in range(2):
            for f in range(FRAMES):
                ebf[s, f, :, 0:OWN] = jnp.zeros((C, OWN), BF)
                ebf[s, f, :, OWN + PX : EXT] = jnp.zeros((C, OWN), BF)

        barrier = pltpu.get_barrier_semaphore()

        def signal(sem, **place):
            pl.semaphore_signal(sem, inc=1, device_id=place, device_id_type=MESH)

        def along_z(d):
            return 2 * (lax.rem(chip_z + d + deep, deep) * wide + chip_y) + core

        def along_y(d):
            return 2 * (chip_z * wide + lax.rem(chip_y + d, wide)) + core

        for d in range(1, columns_of_space):
            signal(barrier, space=lax.rem(space + d, columns_of_space))
        signal(barrier, step=partner)
        for d in range(1, wide):
            signal(barrier, step=along_y(d))
        close = columns_of_space + wide - 1
        if deep > 1:
            signal(barrier, step=along_z(1))
            signal(barrier, step=along_z(-1))
            close += 2

        def greet(n):
            if n < 2 and deep > 1:
                signal(near.at[n], step=along_z(n + 1))
                signal(near.at[n], step=along_z(-n - 1))
            if n == 2:
                for d in range(1, wide):
                    signal(near.at[n], step=along_y(d))

        def greeted(n):
            if n < 2 and deep > 1:
                pl.semaphore_wait(near.at[n], 2)
            if n == 2:
                pl.semaphore_wait(near.at[n], wide - 1)

        lane = lax.broadcasted_iota(jnp.int32, (1, EXT), 1)
        column = lax.rem(lane + (4 * COLS - OWN % COLS), COLS)
        not_last = column != COLS - 1
        not_first = column != 0

        def halo_copies(s, f):
            right = pltpu.make_async_remote_copy(
                src_ref=ebf.at[s, f, :, pl.ds(OWN + PX - 256, 256)],
                dst_ref=ebf.at[s, f, :, pl.ds(0, 256)],
                send_sem=halo_send.at[s, f, 0],
                recv_sem=halo_recv.at[s, f, 0],
                device_id={"space": lax.rem(space + 1, columns_of_space)},
                device_id_type=MESH,
            )
            left = pltpu.make_async_remote_copy(
                src_ref=ebf.at[s, f, :, pl.ds(OWN, 256)],
                dst_ref=ebf.at[s, f, :, pl.ds(OWN + PX, 256)],
                send_sem=halo_send.at[s, f, 1],
                recv_sem=halo_recv.at[s, f, 1],
                device_id={"space": lax.rem(space + columns_of_space - 1, columns_of_space)},
                device_id_type=MESH,
            )
            return right, left

        def half_copies(f):
            ahead = lax.rem(space + 1, columns_of_space)
            behind = lax.rem(space + columns_of_space - 1, columns_of_space)
            pairs = []
            for n, (place, start, landing) in enumerate(
                ((ahead, PX - 256, 0), (behind, 0, OWN + PX))
            ):
                landed = ebf.at[1, f, mine_rows, pl.ds(landing, 256)]
                own_edge = pltpu.make_async_remote_copy(
                    src_ref=ebf.at[1, f, mine_rows, pl.ds(OWN + start, 256)],
                    dst_ref=landed,
                    send_sem=halo_send.at[1, f, n],
                    recv_sem=halo_recv.at[1, f, n],
                    device_id={"space": place},
                    device_id_type=MESH,
                )
                other_edge = pltpu.make_async_remote_copy(
                    src_ref=eob.at[f, :, pl.ds(start, 256)],
                    dst_ref=landed,
                    send_sem=half_send.at[f, n],
                    recv_sem=halo_recv.at[1, f, n],
                    device_id={"space": place, "step": partner},
                    device_id_type=MESH,
                )
                pairs.append((own_edge, other_edge))
            return pairs

        def halo_sends(s, f):
            return half_copies(f) if s == 1 else [(copy,) for copy in halo_copies(s, f)]

        def halo_start(s, f):
            right, left = halo_sends(s, f)

            @pl.when(space < columns_of_space - 1)
            def _():
                for copy in right:
                    copy.start()

            @pl.when(space > 0)
            def _():
                for copy in left:
                    copy.start()

        def halo_wait(s, f):
            right, left = halo_copies(s, f)

            @pl.when(space > 0)
            def _():
                right.wait_recv()

            @pl.when(space < columns_of_space - 1)
            def _():
                left.wait_recv()

        def halo_done(s, f):
            right, left = halo_sends(s, f)

            @pl.when(space < columns_of_space - 1)
            def _():
                for copy in right:
                    copy.wait_send()

            @pl.when(space > 0)
            def _():
                for copy in left:
                    copy.wait_send()

        def im2col(s, f):
            halo_wait(s, f)
            whole = ebf[s, f]
            if s == 1:
                whole = jnp.where(anchor, ebf[0, f], whole)
            zero = jnp.zeros_like(whole)
            shifted = (jnp.where(not_last, whole, zero), whole, jnp.where(not_first, whole, zero))
            for b in range(3):
                for c in range(3):
                    start = Q0 + COLS * (b - 1) + (c - 1)
                    row = f * 9 * C + (b * 3 + c) * C
                    xc[row : row + C, :] = shifted[c][:, start : start + NQ]

        def conv_one(f):
            low, high = max(f - 1, 0), min(f + 2, FRAMES)
            first = low - f + 1
            weights = w1s[:, 9 * C * first : 9 * C * (first + high - low)]
            for n in range(0, NQ, CHUNK):
                m = min(n + CHUNK, NQ)
                value = jnp.dot(
                    weights, xc[low * 9 * C : high * 9 * C, n:m], preferred_element_type=F32
                )
                value = value + jnp.concatenate([temb[...]] * ((m - n) // 128), axis=1)
                value = value / (1.0 + jnp.exp(-value))
                if n + Q0 < OWN:
                    place = lax.broadcasted_iota(jnp.int32, (1, m - n), 1) + (n + Q0)
                    value = jnp.where((place >= OWN) | (space > 0), value, 0.0)
                if m + Q0 > OWN + PX:
                    place = lax.broadcasted_iota(jnp.int32, (1, m - n), 1) + (n + Q0)
                    value = jnp.where(
                        (place < OWN + PX) | (space < columns_of_space - 1), value, 0.0
                    )
                hid[f * HID : (f + 1) * HID, n:m] = value.astype(BF)

        def conv_two(f):
            low, high = max(f - 1, 0), min(f + 2, FRAMES)
            first = low - f + 1
            weights = w2s[:, HID * first : HID * (first + high - low)]
            for n in range(0, NQ, CHUNK):
                m = min(n + CHUNK, NQ)
                grp[f % 2, :, n:m] = jnp.dot(
                    weights, hid[low * HID : high * HID, n:m], preferred_element_type=F32
                )

        def combine(f):
            masks = (not_last[:, Q0 : Q0 + NQ], None, not_first[:, Q0 : Q0 + NQ])
            total = None
            for b in range(3):
                for c in range(3):
                    tap = b * 3 + c
                    value = grp[f % 2, tap * C : (tap + 1) * C, :]
                    if masks[c] is not None:
                        value = jnp.where(masks[c], value, 0.0)
                    start = OWN - Q0 + COLS * (b - 1) + (c - 1)
                    value = pltpu.roll(value, (NQ - start) % NQ, 1)[:, :PX]
                    total = value if total is None else total + value
            return total

        def pair_copy(s, f):
            return pltpu.make_async_remote_copy(
                src_ref=st.at[s, f, other_rows, :],
                dst_ref=pb.at[s, f],
                send_sem=pair_send.at[s, f],
                recv_sem=pair_recv.at[s, f],
                device_id={"step": partner},
                device_id_type=MESH,
            )

        def drift(s, f):
            latent = ent[s, f]
            value = decay_gain * latent + noise_gain * combine(f) + spread_gain * noise[f]
            st[s, f] = value + jnp.where(anchor, latent, 0.0)
            pair_copy(s, f).start()

        def chip_sum(s, f):
            pair_copy(s, f).wait_recv()
            total = st[s, f, mine_rows, :] + pb[s, f]
            for r in range(HALF // 8):
                for b in range(BLOCKS):
                    cs[s, f, r * BLOCKS + b] = total[8 * r : 8 * r + 8, 128 * b : 128 * b + 128]
            for k in range(parts):
                low, high, base = span(f, k)

                for g in range(low, high):
                    owner = (g + base) % chips
                    own_tile = chip == owner
                    pltpu.make_async_remote_copy(
                        src_ref=cs.at[s, f, g],
                        dst_ref=rx.at[s, f, k, jnp.where(own_tile, chips, chip)],
                        send_sem=cs_send.at[s, f, k],
                        recv_sem=rx_recv.at[s, f, k],
                        device_id={"step": jnp.where(own_tile, partner, 2 * owner + core)},
                        device_id_type=MESH,
                    ).start()

                def keep(g):
                    rx[s, f, k, chip] = cs[s, f, g]

                if_mine(f, k, keep)

        def own(s, f):
            for k in range(parts):

                def work(g):
                    given = rx.at[s, f, k, pl.ds(0, chips)]
                    pltpu.make_async_copy(given, given, rx_recv.at[s, f, k]).wait()
                    running = jnp.zeros((8, 128), F32)
                    for q in range(chips):
                        tx[s, f, k, q] = running
                        running = running + rx[s, f, k, q]

                    @pl.loop(far, far + chips - 1)
                    def _(d):
                        target = chip + jnp.where(d >= chips, d - chips + 1, d)
                        target = jnp.where(target >= chips, target - chips, target)
                        pltpu.make_async_remote_copy(
                            src_ref=tx.at[s, f, k, target],
                            dst_ref=px.at[s, f, g],
                            send_sem=tx_send.at[s, f, k],
                            recv_sem=px_recv.at[s, f, k],
                            device_id={"step": 2 * target + core},
                            device_id_type=MESH,
                        ).start()

                    px[s, f, g] = tx[s, f, k, chip]

                if_mine(f, k, work)

        def span(f, k):
            low, high = k * chips, min((k + 1) * chips, TILES)
            return low, high, f * TILES % chips - low

        def if_mine(f, k, work, otherwise=None):
            low, high, base = span(f, k)
            g = chip - base
            g = jnp.where(g < low, g + chips, g)
            if high - low == chips:
                work(g)
            else:
                pl.when(g < high)(lambda: work(g))
                if otherwise is not None:
                    pl.when(g >= high)(lambda: otherwise(g))

        def tiles_wait(ref, sem, s, f):
            for k in range(parts):
                low, high, _ = span(f, k)

                def wait(count):
                    tiles = ref.at[s, f, pl.ds(0, count)]
                    return lambda g: pltpu.make_async_copy(tiles, tiles, sem.at[s, f, k]).wait()

                if_mine(f, k, wait(high - low - 1), wait(high - low))

        def scan_done(s, f):
            for k in range(parts):
                low, high, _ = span(f, k)
                tiles = cs.at[s, f, pl.ds(low, high - low)]
                pltpu.make_async_copy(tiles, tiles, cs_send.at[s, f, k]).wait()

                def wait(g):
                    sent = tx.at[s, f, k, pl.ds(0, chips - 1)]
                    pltpu.make_async_copy(sent, sent, tx_send.at[s, f, k]).wait()

                if_mine(f, k, wait)

        def enter_copy(s, f):
            return pltpu.make_async_remote_copy(
                src_ref=eo.at[s, f],
                dst_ref=ent.at[s + 1, f, mine_rows, :],
                send_sem=eo_send.at[s, f],
                recv_sem=ent_recv.at[s, f],
                device_id={"step": partner},
                device_id_type=MESH,
            )

        def enter(s, f):
            tiles_wait(px, px_recv, s, f)
            before = jnp.concatenate(
                [
                    jnp.concatenate(
                        [px[s, f, r * BLOCKS + b] for b in range(BLOCKS)], axis=1
                    )
                    for r in range(HALF // 8)
                ],
                axis=0,
            )
            first = jnp.where(core == 0, st[s, f, mine_rows, :], pb[s, f])
            after = before + first
            own_part = jnp.where(core == 0, before, after)
            other_part = jnp.where(core == 0, after, before)
            eo[s, f] = other_part
            enter_copy(s, f).start()
            ent[s + 1, f, mine_rows, :] = own_part
            if s == 0:
                ebf[1, f, mine_rows, OWN : OWN + PX] = own_part.astype(BF)
                eob[f] = other_part.astype(BF)
                halo_start(1, f)
                return None
            first_step = chip == 0
            squares = []
            for keep_from, now, was, now_step, was_step in (
                (anchor, own_part, ent[1, f, mine_rows, :], st[1, f, mine_rows, :], st[0, f, mine_rows, :]),
                (first_step & (core == 1), other_part, eo[0, f], pb[1, f], pb[0, f]),
            ):
                keep = jnp.where(keep_from, 0.0, 1.0)
                change = (keep * now + now_step) - (keep * was + was_step)
                change = change * change
                square = None
                for r in range(HALF // 8):
                    for b in range(BLOCKS):
                        part = change[8 * r : 8 * r + 8, 128 * b : 128 * b + 128]
                        square = part if square is None else square + part
                squares.append(square)
            return squares

        def entered(s, f):
            theirs = ent.at[s + 1, f, other_rows, :]
            pltpu.make_async_copy(theirs, theirs, ent_recv.at[s, f]).wait()
            if s == 0:
                ebf[1, f, other_rows, OWN : OWN + PX] = ent[1, f, other_rows, :].astype(BF)

            @pl.when(anchor)
            def _():
                ent[s + 1, f] = ent[0, f]

        def sum_copy(n, d):
            place = {"space": lax.rem(space + d, columns_of_space)}
            if n == 1:
                place["step"] = partner
            return pltpu.make_async_remote_copy(
                src_ref=ssq.at[n],
                dst_ref=red.at[core, space],
                send_sem=red_send.at[n, d],
                recv_sem=red_recv.at[core, space],
                device_id=place,
                device_id_type=MESH,
            )

        sums = [(0, d) for d in range(1, columns_of_space)]
        sums += [(1, d) for d in range(columns_of_space)]

        for copy in loads[:FRAMES]:
            copy.wait()
        for f in range(FRAMES):
            ebf[0, f, :, OWN : OWN + PX] = ent[0, f].astype(BF)

        pl.semaphore_wait(barrier, close)
        greet(0)
        for f in range(FRAMES):
            halo_start(0, f)

        before = jnp.full((8, 128), times[0, 0], jnp.int32).astype(F32)
        after = jnp.full((8, 128), times[0, 1], jnp.int32).astype(F32)
        decay_gain, noise_gain, spread_gain = [
            gain[0:1, 0:1] for gain in coefficients(before, after)
        ]
        index = lax.broadcasted_iota(jnp.int32, (C, 128), 0)
        sine = index < C // 2
        place = jnp.where(sine, index, index - C // 2).astype(F32)
        frequency = jnp.exp(-math.log(10000.0) * place / (C // 2))
        angles = before[0:1, :] * frequency
        features = jnp.where(sine, jnp.sin(angles), jnp.cos(angles))
        late[0].wait()
        for n in range(0, HID, 128):
            row = jnp.sum(twr[:, n : n + 128] * features, axis=0, keepdims=True)
            temb[n : n + 128, :] = jnp.broadcast_to(row, (128, 128)).T
        late[1].wait()
        for n in range(0, 27 * C, 128):
            m = min(n + 128, 27 * C)
            w1s[:, n:m] = w1r[n:m, :].T
        late[2].wait()
        for a in range(3):
            for tap in range(9):
                w2s[tap * C : (tap + 1) * C, a * HID : (a + 1) * HID] = w2r[
                    a, :, tap * HID : (tap + 1) * HID
                ]
        for copy in loads[FRAMES:]:
            copy.wait()

        def out_copy(f):
            return pltpu.make_async_copy(res.at[f], out_hbm.at[:, f, :], out_sem.at[f])

        for s in range(2):
            im2col(s, 0)
            im2col(s, 1)
            if s == 0:
                greeted(0)
                greet(1)
            conv_one(0)
            im2col(s, 2)
            if s == 0:
                greeted(1)
                greet(2)
            conv_one(1)
            conv_two(0)
            drift(s, 0)
            im2col(s, 3)
            conv_one(2)
            if s == 0:
                greeted(2)
            chip_sum(s, 0)
            conv_two(1)
            conv_one(3)
            drift(s, 1)
            conv_two(2)
            conv_two(3)
            drift(s, 2)
            chip_sum(s, 1)
            drift(s, 3)
            chip_sum(s, 2)
            chip_sum(s, 3)
            for f in range(FRAMES):
                own(s, f)
            squares = [enter(s, 0)]
            for f in range(FRAMES):
                if f + 1 < FRAMES:
                    squares.append(enter(s, f + 1))
                if s == 1 and f + 2 == FRAMES:
                    for n in range(2):
                        ssq[n] = squares[0][n] + squares[1][n] + squares[2][n] + squares[3][n]
                    red[core, space] = ssq[0]
                    for n, d in sums:
                        sum_copy(n, d).start()
                entered(s, f)
                if s == 1:
                    res[f] = jnp.where(anchor, 0.0, 1.0) * ent[2, f] + st[1, f]
                    out_copy(f).start()

        for s in range(2):
            for f in range(FRAMES):
                halo_done(s, f)
                pair_copy(s, f).wait_send()
                enter_copy(s, f).wait_send()
                scan_done(s, f)
        for f in range(FRAMES):
            out_copy(f).wait()

        for n, d in sums:
            sum_copy(n, d).wait_send()
        for n, d in sums:
            given = (core if n == 0 else other, lax.rem(space + d, columns_of_space))
            cells = red.at[given]
            pltpu.make_async_copy(cells, cells, red_recv.at[given]).wait()
        total = None
        for n in range(2):
            for x in range(columns_of_space):
                total = red[n, x] if total is None else total + red[n, x]
        mean = jnp.full((8, 128), jnp.sum(total), F32) / cell_count
        chg_ref[0] = jnp.max(jnp.sqrt(mean))

    scratch = [
        pltpu.VMEM((3, FRAMES, C, PX), F32),
        pltpu.VMEM((2, FRAMES, C, EXT), BF),
        pltpu.VMEM((FRAMES * 9 * C, NQ), BF),
        pltpu.VMEM((FRAMES * HID, NQ), BF),
        pltpu.VMEM((2, 9 * C, NQ), F32),
        pltpu.VMEM((27 * C, HID), BF),
        pltpu.VMEM((3, C, 9 * HID), BF),
        pltpu.VMEM((C, HID), F32),
        pltpu.VMEM((HID, 27 * C), BF),
        pltpu.VMEM((9 * C, 3 * HID), BF),
        pltpu.VMEM((HID, 128), F32),
        pltpu.VMEM((FRAMES, C, PX), F32),
        pltpu.VMEM((FRAMES, C, PX), F32),
        pltpu.VMEM((2, FRAMES, C, PX), F32),
        pltpu.VMEM((2, FRAMES, HALF, PX), F32),
        pltpu.VMEM((2, FRAMES, TILES, 8, 128), F32),
        pltpu.VMEM((2, FRAMES, parts, chips + 1, 8, 128), F32),
        pltpu.VMEM((2, FRAMES, parts, chips, 8, 128), F32),
        pltpu.VMEM((2, FRAMES, TILES, 8, 128), F32),
        pltpu.VMEM((2, FRAMES, HALF, PX), F32),
        pltpu.VMEM((FRAMES, HALF, PX), BF),
        pltpu.VMEM((2, 8, 128), F32),
        pltpu.VMEM((2, columns_of_space, 8, 128), F32),
        pltpu.SemaphoreType.DMA((2 * FRAMES + 3,)),
        pltpu.SemaphoreType.DMA((FRAMES,)),
        pltpu.SemaphoreType.REGULAR((3,)),
        pltpu.SemaphoreType.DMA((2, FRAMES, 2)),
        pltpu.SemaphoreType.DMA((2, FRAMES, 2)),
        pltpu.SemaphoreType.DMA((2, FRAMES)),
        pltpu.SemaphoreType.DMA((2, FRAMES)),
        pltpu.SemaphoreType.DMA((2, FRAMES, parts)),
        pltpu.SemaphoreType.DMA((2, FRAMES, parts)),
        pltpu.SemaphoreType.DMA((2, FRAMES, parts)),
        pltpu.SemaphoreType.DMA((2, FRAMES, parts)),
        pltpu.SemaphoreType.DMA((2, FRAMES)),
        pltpu.SemaphoreType.DMA((2, FRAMES)),
        pltpu.SemaphoreType.DMA((FRAMES, 2)),
        pltpu.SemaphoreType.DMA((2, columns_of_space)),
        pltpu.SemaphoreType.DMA((2, columns_of_space)),
    ]
    return kernel, scratch


def solution(mesh):
    steps, spaces = mesh.shape["step"], mesh.shape["space"]
    cell_count = float(C * FRAMES * PX * spaces)
    kernel, scratch = make_kernel(steps // 2, spaces, cell_count)

    def local(guesses, noise, timesteps, conv_first, conv_second, time_weight):
        anywhere = pl.BlockSpec(memory_space=pl.ANY)
        scalars = pl.BlockSpec(memory_space=pltpu.SMEM)
        first = conv_first.transpose(0, 2, 1).reshape(27 * C, HID)
        states, changes = pl.pallas_call(
            kernel,
            out_shape=(
                jax.ShapeDtypeStruct((C, FRAMES, PX), F32),
                jax.ShapeDtypeStruct((1,), F32),
            ),
            in_specs=[scalars] + [anywhere] * 5,
            out_specs=(anywhere, scalars),
            scratch_shapes=scratch,
            compiler_params=pltpu.CompilerParams(
                collective_id=0, has_side_effects=True, vmem_limit_bytes=56 * 2**20
            ),
        )(timesteps, guesses[0], noise[0], first, conv_second, time_weight)
        return states[None], changes

    in_specs = (
        P("step", None, None, "space"),
        P("step", None, None, "space"),
        P("step", None),
        P(),
        P(),
        P(),
    )
    out_specs = (P("step", None, None, "space"), P("step"))
    return jax.shard_map(local, mesh=mesh, in_specs=in_specs, out_specs=out_specs, check_vma=False)
```

```python
import math

import jax
import jax.numpy as jnp
from jax import lax
from jax.experimental import pallas as pl
from jax.experimental.pallas import tpu as pltpu
from jax.sharding import PartitionSpec as P

C = 64
HID = 256
COLS = 80
FRAMES = 4
BF = jnp.bfloat16
F32 = jnp.float32
MESH = pl.DeviceIdType.MESH

PX = 640
OWN = 256
EXT = OWN + PX + 256
Q0 = 128
NQ = 896
HALF = C // 2
TILES = HALF // 8 * (PX // 128)
BLOCKS = PX // 128
CHUNK = 256


def expm1(value):
    series = 1.0 + value / 11.0
    for n in range(10, 1, -1):
        series = 1.0 + value / n * series
    return jnp.where(jnp.abs(value) < 0.5, value * series, jnp.exp(value) - 1.0)


def plan(timestep):
    scaled = timestep / 1000.0
    return -(0.1 * scaled + 9.95 * scaled * scaled)


def coefficients(before, after):
    log_from = plan(before)
    log_to = plan(after)
    half_gap = 0.5 * (log_to - log_from)
    decay_gain = expm1(half_gap)
    remain_from = -expm1(log_from)
    remain_to = -expm1(log_to)
    ratio_term = -expm1(log_from - log_to)
    noise_gain = -jnp.exp(half_gap) * jnp.sqrt(remain_from) + remain_to * jnp.exp(
        -half_gap
    ) / jnp.sqrt(remain_from)
    spread_gain = jnp.sqrt(remain_to / remain_from * ratio_term)
    return decay_gain, noise_gain, spread_gain


def make_kernel(chips, columns_of_space, cell_count):
    parts = -(-TILES // chips)
    wide = min(4, chips)
    deep = chips // wide
    far = max(1, chips // 2 - 2)

    def kernel(
        times, y_hbm, n_hbm, w1_hbm, w2_hbm, tw_hbm, out_hbm, chg_ref,
        ent, ebf, xc, hid, grp, w1r, w2r, twr, w1s, w2s, temb, noise, res,
        st, pb, cs, rx, tx, px, eo, eob, ssq, red, load_sem, out_sem, near,
        halo_send, halo_recv, pair_send, pair_recv, cs_send, rx_recv, tx_send, px_recv,
        eo_send, ent_recv, half_send, red_send, red_recv,
    ):
        step = lax.axis_index("step")
        space = lax.axis_index("space")
        chip = step // 2
        core = step - 2 * chip
        chip_z = chip // wide
        chip_y = chip - chip_z * wide
        other = 1 - core
        partner = 2 * chip + other
        anchor = step == 0
        mine_rows = pl.ds(pl.multiple_of(core * HALF, HALF), HALF)
        other_rows = pl.ds(pl.multiple_of(other * HALF, HALF), HALF)

        loads = [pltpu.make_async_copy(y_hbm.at[:, f, :], ent.at[0, f], load_sem.at[f]) for f in range(FRAMES)]
        loads += [
            pltpu.make_async_copy(n_hbm.at[:, f, :], noise.at[f], load_sem.at[FRAMES + f])
            for f in range(FRAMES)
        ]
        late = [
            pltpu.make_async_copy(tw_hbm, twr, load_sem.at[2 * FRAMES]),
            pltpu.make_async_copy(w1_hbm, w1r, load_sem.at[2 * FRAMES + 1]),
            pltpu.make_async_copy(w2_hbm, w2r, load_sem.at[2 * FRAMES + 2]),
        ]
        for copy in loads[:FRAMES] + late:
            copy.start()

        for s in range(2):
            for f in range(FRAMES):
                ebf[s, f, :, 0:OWN] = jnp.zeros((C, OWN), BF)
                ebf[s, f, :, OWN + PX : EXT] = jnp.zeros((C, OWN), BF)

        barrier = pltpu.get_barrier_semaphore()

        def signal(sem, **place):
            pl.semaphore_signal(sem, inc=1, device_id=place, device_id_type=MESH)

        def along_z(d):
            return 2 * (lax.rem(chip_z + d + deep, deep) * wide + chip_y) + core

        def along_y(d):
            return 2 * (chip_z * wide + lax.rem(chip_y + d, wide)) + core

        for d in range(1, columns_of_space):
            signal(barrier, space=lax.rem(space + d, columns_of_space))
        signal(barrier, step=partner)
        for d in range(1, wide):
            signal(barrier, step=along_y(d))
        close = columns_of_space + wide - 1
        if deep > 1:
            signal(barrier, step=along_z(1))
            signal(barrier, step=along_z(-1))
            close += 2

        def greet(n):
            if n < 2 and deep > 1:
                signal(near.at[n], step=along_z(n + 1))
                signal(near.at[n], step=along_z(-n - 1))
            if n == 2:
                for d in range(1, wide):
                    signal(near.at[n], step=along_y(d))

        def greeted(n):
            if n < 2 and deep > 1:
                pl.semaphore_wait(near.at[n], 2)
            if n == 2:
                pl.semaphore_wait(near.at[n], wide - 1)

        lane = lax.broadcasted_iota(jnp.int32, (1, EXT), 1)
        column = lax.rem(lane + (4 * COLS - OWN % COLS), COLS)
        not_last = column != COLS - 1
        not_first = column != 0

        def halo_copies(s, f):
            right = pltpu.make_async_remote_copy(
                src_ref=ebf.at[s, f, :, pl.ds(OWN + PX - 256, 256)],
                dst_ref=ebf.at[s, f, :, pl.ds(0, 256)],
                send_sem=halo_send.at[s, f, 0],
                recv_sem=halo_recv.at[s, f, 0],
                device_id={"space": lax.rem(space + 1, columns_of_space)},
                device_id_type=MESH,
            )
            left = pltpu.make_async_remote_copy(
                src_ref=ebf.at[s, f, :, pl.ds(OWN, 256)],
                dst_ref=ebf.at[s, f, :, pl.ds(OWN + PX, 256)],
                send_sem=halo_send.at[s, f, 1],
                recv_sem=halo_recv.at[s, f, 1],
                device_id={"space": lax.rem(space + columns_of_space - 1, columns_of_space)},
                device_id_type=MESH,
            )
            return right, left

        def half_copies(f):
            ahead = lax.rem(space + 1, columns_of_space)
            behind = lax.rem(space + columns_of_space - 1, columns_of_space)
            pairs = []
            for n, (place, start, landing) in enumerate(
                ((ahead, PX - 256, 0), (behind, 0, OWN + PX))
            ):
                landed = ebf.at[1, f, mine_rows, pl.ds(landing, 256)]
                own_edge = pltpu.make_async_remote_copy(
                    src_ref=ebf.at[1, f, mine_rows, pl.ds(OWN + start, 256)],
                    dst_ref=landed,
                    send_sem=halo_send.at[1, f, n],
                    recv_sem=halo_recv.at[1, f, n],
                    device_id={"space": place},
                    device_id_type=MESH,
                )
                other_edge = pltpu.make_async_remote_copy(
                    src_ref=eob.at[f, :, pl.ds(start, 256)],
                    dst_ref=landed,
                    send_sem=half_send.at[f, n],
                    recv_sem=halo_recv.at[1, f, n],
                    device_id={"space": place, "step": partner},
                    device_id_type=MESH,
                )
                pairs.append((own_edge, other_edge))
            return pairs

        def halo_sends(s, f):
            return half_copies(f) if s == 1 else [(copy,) for copy in halo_copies(s, f)]

        def halo_start(s, f):
            right, left = halo_sends(s, f)

            @pl.when(space < columns_of_space - 1)
            def _():
                for copy in right:
                    copy.start()

            @pl.when(space > 0)
            def _():
                for copy in left:
                    copy.start()

        def halo_wait(s, f):
            right, left = halo_copies(s, f)

            @pl.when(space > 0)
            def _():
                right.wait_recv()

            @pl.when(space < columns_of_space - 1)
            def _():
                left.wait_recv()

        def halo_done(s, f):
            right, left = halo_sends(s, f)

            @pl.when(space < columns_of_space - 1)
            def _():
                for copy in right:
                    copy.wait_send()

            @pl.when(space > 0)
            def _():
                for copy in left:
                    copy.wait_send()

        def im2col(s, f):
            halo_wait(s, f)
            whole = ebf[s, f]
            if s == 1:
                whole = jnp.where(anchor, ebf[0, f], whole)
            zero = jnp.zeros_like(whole)
            shifted = (jnp.where(not_last, whole, zero), whole, jnp.where(not_first, whole, zero))
            for b in range(3):
                for c in range(3):
                    start = Q0 + COLS * (b - 1) + (c - 1)
                    row = f * 9 * C + (b * 3 + c) * C
                    xc[row : row + C, :] = shifted[c][:, start : start + NQ]

        def conv_one(f):
            low, high = max(f - 1, 0), min(f + 2, FRAMES)
            first = low - f + 1
            weights = w1s[:, 9 * C * first : 9 * C * (first + high - low)]
            for n in range(0, NQ, CHUNK):
                m = min(n + CHUNK, NQ)
                value = jnp.dot(
                    weights, xc[low * 9 * C : high * 9 * C, n:m], preferred_element_type=F32
                )
                value = value + jnp.concatenate([temb[...]] * ((m - n) // 128), axis=1)
                value = value / (1.0 + jnp.exp(-value))
                if n + Q0 < OWN:
                    place = lax.broadcasted_iota(jnp.int32, (1, m - n), 1) + (n + Q0)
                    value = jnp.where((place >= OWN) | (space > 0), value, 0.0)
                if m + Q0 > OWN + PX:
                    place = lax.broadcasted_iota(jnp.int32, (1, m - n), 1) + (n + Q0)
                    value = jnp.where(
                        (place < OWN + PX) | (space < columns_of_space - 1), value, 0.0
                    )
                hid[f * HID : (f + 1) * HID, n:m] = value.astype(BF)

        def conv_two(f):
            low, high = max(f - 1, 0), min(f + 2, FRAMES)
            first = low - f + 1
            weights = w2s[:, HID * first : HID * (first + high - low)]
            for n in range(0, NQ, CHUNK):
                m = min(n + CHUNK, NQ)
                grp[f % 2, :, n:m] = jnp.dot(
                    weights, hid[low * HID : high * HID, n:m], preferred_element_type=F32
                )

        def combine(f):
            masks = (not_last[:, Q0 : Q0 + NQ], None, not_first[:, Q0 : Q0 + NQ])
            total = None
            for b in range(3):
                for c in range(3):
                    tap = b * 3 + c
                    value = grp[f % 2, tap * C : (tap + 1) * C, :]
                    if masks[c] is not None:
                        value = jnp.where(masks[c], value, 0.0)
                    start = OWN - Q0 + COLS * (b - 1) + (c - 1)
                    value = pltpu.roll(value, (NQ - start) % NQ, 1)[:, :PX]
                    total = value if total is None else total + value
            return total

        def pair_copy(s, f):
            return pltpu.make_async_remote_copy(
                src_ref=st.at[s, f, other_rows, :],
                dst_ref=pb.at[s, f],
                send_sem=pair_send.at[s, f],
                recv_sem=pair_recv.at[s, f],
                device_id={"step": partner},
                device_id_type=MESH,
            )

        def drift(s, f):
            latent = ent[s, f]
            value = decay_gain * latent + noise_gain * combine(f) + spread_gain * noise[f]
            st[s, f] = value + jnp.where(anchor, latent, 0.0)
            pair_copy(s, f).start()

        def chip_sum(s, f):
            pair_copy(s, f).wait_recv()
            total = st[s, f, mine_rows, :] + pb[s, f]
            for r in range(HALF // 8):
                for b in range(BLOCKS):
                    cs[s, f, r * BLOCKS + b] = total[8 * r : 8 * r + 8, 128 * b : 128 * b + 128]
            for k in range(parts):
                low, high, base = span(f, k)

                for g in range(low, high):
                    owner = (g + base) % chips
                    own_tile = chip == owner
                    pltpu.make_async_remote_copy(
                        src_ref=cs.at[s, f, g],
                        dst_ref=rx.at[s, f, k, jnp.where(own_tile, chips, chip)],
                        send_sem=cs_send.at[s, f, k],
                        recv_sem=rx_recv.at[s, f, k],
                        device_id={"step": jnp.where(own_tile, partner, 2 * owner + core)},
                        device_id_type=MESH,
                    ).start()

                def keep(g):
                    rx[s, f, k, chip] = cs[s, f, g]

                if_mine(f, k, keep)

        def own(s, f):
            for k in range(parts):

                def work(g):
                    given = rx.at[s, f, k, pl.ds(0, chips)]
                    pltpu.make_async_copy(given, given, rx_recv.at[s, f, k]).wait()
                    running = jnp.zeros((8, 128), F32)
                    for q in range(chips):
                        tx[s, f, k, q] = running
                        running = running + rx[s, f, k, q]

                    @pl.loop(far, far + chips - 1)
                    def _(d):
                        target = chip + jnp.where(d >= chips, d - chips + 1, d)
                        target = jnp.where(target >= chips, target - chips, target)
                        pltpu.make_async_remote_copy(
                            src_ref=tx.at[s, f, k, target],
                            dst_ref=px.at[s, f, g],
                            send_sem=tx_send.at[s, f, k],
                            recv_sem=px_recv.at[s, f, k],
                            device_id={"step": 2 * target + core},
                            device_id_type=MESH,
                        ).start()

                    px[s, f, g] = tx[s, f, k, chip]

                if_mine(f, k, work)

        def span(f, k):
            low, high = k * chips, min((k + 1) * chips, TILES)
            return low, high, f * TILES % chips - low

        def if_mine(f, k, work, otherwise=None):
            low, high, base = span(f, k)
            g = chip - base
            g = jnp.where(g < low, g + chips, g)
            if high - low == chips:
                work(g)
            else:
                pl.when(g < high)(lambda: work(g))
                if otherwise is not None:
                    pl.when(g >= high)(lambda: otherwise(g))

        def tiles_wait(ref, sem, s, f):
            for k in range(parts):
                low, high, _ = span(f, k)

                def wait(count):
                    tiles = ref.at[s, f, pl.ds(0, count)]
                    return lambda g: pltpu.make_async_copy(tiles, tiles, sem.at[s, f, k]).wait()

                if_mine(f, k, wait(high - low - 1), wait(high - low))

        def scan_done(s, f):
            for k in range(parts):
                low, high, _ = span(f, k)
                tiles = cs.at[s, f, pl.ds(low, high - low)]
                pltpu.make_async_copy(tiles, tiles, cs_send.at[s, f, k]).wait()

                def wait(g):
                    sent = tx.at[s, f, k, pl.ds(0, chips - 1)]
                    pltpu.make_async_copy(sent, sent, tx_send.at[s, f, k]).wait()

                if_mine(f, k, wait)

        def enter_copy(s, f):
            return pltpu.make_async_remote_copy(
                src_ref=eo.at[s, f],
                dst_ref=ent.at[s + 1, f, mine_rows, :],
                send_sem=eo_send.at[s, f],
                recv_sem=ent_recv.at[s, f],
                device_id={"step": partner},
                device_id_type=MESH,
            )

        def enter(s, f):
            tiles_wait(px, px_recv, s, f)
            before = jnp.concatenate(
                [
                    jnp.concatenate(
                        [px[s, f, r * BLOCKS + b] for b in range(BLOCKS)], axis=1
                    )
                    for r in range(HALF // 8)
                ],
                axis=0,
            )
            first = jnp.where(core == 0, st[s, f, mine_rows, :], pb[s, f])
            after = before + first
            own_part = jnp.where(core == 0, before, after)
            other_part = jnp.where(core == 0, after, before)
            eo[s, f] = other_part
            enter_copy(s, f).start()
            ent[s + 1, f, mine_rows, :] = own_part
            if s == 0:
                ebf[1, f, mine_rows, OWN : OWN + PX] = own_part.astype(BF)
                eob[f] = other_part.astype(BF)
                halo_start(1, f)
                return None
            first_step = chip == 0
            squares = []
            for keep_from, now, was, now_step, was_step in (
                (anchor, own_part, ent[1, f, mine_rows, :], st[1, f, mine_rows, :], st[0, f, mine_rows, :]),
                (first_step & (core == 1), other_part, eo[0, f], pb[1, f], pb[0, f]),
            ):
                keep = jnp.where(keep_from, 0.0, 1.0)
                change = (keep * now + now_step) - (keep * was + was_step)
                change = change * change
                square = None
                for r in range(HALF // 8):
                    for b in range(BLOCKS):
                        part = change[8 * r : 8 * r + 8, 128 * b : 128 * b + 128]
                        square = part if square is None else square + part
                squares.append(square)
            return squares

        def entered(s, f):
            theirs = ent.at[s + 1, f, other_rows, :]
            pltpu.make_async_copy(theirs, theirs, ent_recv.at[s, f]).wait()
            if s == 0:
                ebf[1, f, other_rows, OWN : OWN + PX] = ent[1, f, other_rows, :].astype(BF)

            @pl.when(anchor)
            def _():
                ent[s + 1, f] = ent[0, f]

        def sum_copy(n, d):
            place = {"space": lax.rem(space + d, columns_of_space)}
            if n == 1:
                place["step"] = partner
            return pltpu.make_async_remote_copy(
                src_ref=ssq.at[n],
                dst_ref=red.at[core, space],
                send_sem=red_send.at[n, d],
                recv_sem=red_recv.at[core, space],
                device_id=place,
                device_id_type=MESH,
            )

        sums = [(0, d) for d in range(1, columns_of_space)]
        sums += [(1, d) for d in range(columns_of_space)]

        for copy in loads[:FRAMES]:
            copy.wait()
        for f in range(FRAMES):
            ebf[0, f, :, OWN : OWN + PX] = ent[0, f].astype(BF)

        pl.semaphore_wait(barrier, close)
        greet(0)
        for f in range(FRAMES):
            halo_start(0, f)
        for copy in loads[FRAMES:]:
            copy.start()

        before = jnp.full((8, 128), times[0, 0], jnp.int32).astype(F32)
        after = jnp.full((8, 128), times[0, 1], jnp.int32).astype(F32)
        decay_gain, noise_gain, spread_gain = [
            gain[0:1, 0:1] for gain in coefficients(before, after)
        ]
        index = lax.broadcasted_iota(jnp.int32, (C, 128), 0)
        sine = index < C // 2
        place = jnp.where(sine, index, index - C // 2).astype(F32)
        frequency = jnp.exp(-math.log(10000.0) * place / (C // 2))
        angles = before[0:1, :] * frequency
        features = jnp.where(sine, jnp.sin(angles), jnp.cos(angles))
        late[0].wait()
        for n in range(0, HID, 128):
            row = jnp.sum(twr[:, n : n + 128] * features, axis=0, keepdims=True)
            temb[n : n + 128, :] = jnp.broadcast_to(row, (128, 128)).T
        late[1].wait()
        for n in range(0, 27 * C, 128):
            m = min(n + 128, 27 * C)
            w1s[:, n:m] = w1r[n:m, :].T
        late[2].wait()
        for a in range(3):
            for tap in range(9):
                w2s[tap * C : (tap + 1) * C, a * HID : (a + 1) * HID] = w2r[
                    a, :, tap * HID : (tap + 1) * HID
                ]

        def out_copy(f):
            return pltpu.make_async_copy(res.at[f], out_hbm.at[:, f, :], out_sem.at[f])

        for s in range(2):
            im2col(s, 0)
            im2col(s, 1)
            if s == 0:
                greeted(0)
                greet(1)
            conv_one(0)
            im2col(s, 2)
            if s == 0:
                greeted(1)
                greet(2)
            conv_one(1)
            conv_two(0)
            if s == 0:
                for copy in loads[FRAMES:]:
                    copy.wait()
            drift(s, 0)
            im2col(s, 3)
            conv_one(2)
            if s == 0:
                greeted(2)
            chip_sum(s, 0)
            conv_two(1)
            conv_one(3)
            drift(s, 1)
            conv_two(2)
            conv_two(3)
            drift(s, 2)
            chip_sum(s, 1)
            drift(s, 3)
            chip_sum(s, 2)
            chip_sum(s, 3)
            for f in range(FRAMES):
                own(s, f)
            squares = [enter(s, 0)]
            for f in range(FRAMES):
                if f + 1 < FRAMES:
                    squares.append(enter(s, f + 1))
                if s == 1 and f + 2 == FRAMES:
                    for n in range(2):
                        ssq[n] = squares[0][n] + squares[1][n] + squares[2][n] + squares[3][n]
                    red[core, space] = ssq[0]
                    for n, d in sums:
                        sum_copy(n, d).start()
                entered(s, f)
                if s == 1:
                    res[f] = jnp.where(anchor, 0.0, 1.0) * ent[2, f] + st[1, f]
                    out_copy(f).start()

        for s in range(2):
            for f in range(FRAMES):
                halo_done(s, f)
                pair_copy(s, f).wait_send()
                enter_copy(s, f).wait_send()
                scan_done(s, f)
        for f in range(FRAMES):
            out_copy(f).wait()

        for n, d in sums:
            sum_copy(n, d).wait_send()
        for n, d in sums:
            given = (core if n == 0 else other, lax.rem(space + d, columns_of_space))
            cells = red.at[given]
            pltpu.make_async_copy(cells, cells, red_recv.at[given]).wait()
        total = None
        for n in range(2):
            for x in range(columns_of_space):
                total = red[n, x] if total is None else total + red[n, x]
        mean = jnp.full((8, 128), jnp.sum(total), F32) / cell_count
        chg_ref[0] = jnp.max(jnp.sqrt(mean))

    scratch = [
        pltpu.VMEM((3, FRAMES, C, PX), F32),
        pltpu.VMEM((2, FRAMES, C, EXT), BF),
        pltpu.VMEM((FRAMES * 9 * C, NQ), BF),
        pltpu.VMEM((FRAMES * HID, NQ), BF),
        pltpu.VMEM((2, 9 * C, NQ), F32),
        pltpu.VMEM((27 * C, HID), BF),
        pltpu.VMEM((3, C, 9 * HID), BF),
        pltpu.VMEM((C, HID), F32),
        pltpu.VMEM((HID, 27 * C), BF),
        pltpu.VMEM((9 * C, 3 * HID), BF),
        pltpu.VMEM((HID, 128), F32),
        pltpu.VMEM((FRAMES, C, PX), F32),
        pltpu.VMEM((FRAMES, C, PX), F32),
        pltpu.VMEM((2, FRAMES, C, PX), F32),
        pltpu.VMEM((2, FRAMES, HALF, PX), F32),
        pltpu.VMEM((2, FRAMES, TILES, 8, 128), F32),
        pltpu.VMEM((2, FRAMES, parts, chips + 1, 8, 128), F32),
        pltpu.VMEM((2, FRAMES, parts, chips, 8, 128), F32),
        pltpu.VMEM((2, FRAMES, TILES, 8, 128), F32),
        pltpu.VMEM((2, FRAMES, HALF, PX), F32),
        pltpu.VMEM((FRAMES, HALF, PX), BF),
        pltpu.VMEM((2, 8, 128), F32),
        pltpu.VMEM((2, columns_of_space, 8, 128), F32),
        pltpu.SemaphoreType.DMA((2 * FRAMES + 3,)),
        pltpu.SemaphoreType.DMA((FRAMES,)),
        pltpu.SemaphoreType.REGULAR((3,)),
        pltpu.SemaphoreType.DMA((2, FRAMES, 2)),
        pltpu.SemaphoreType.DMA((2, FRAMES, 2)),
        pltpu.SemaphoreType.DMA((2, FRAMES)),
        pltpu.SemaphoreType.DMA((2, FRAMES)),
        pltpu.SemaphoreType.DMA((2, FRAMES, parts)),
        pltpu.SemaphoreType.DMA((2, FRAMES, parts)),
        pltpu.SemaphoreType.DMA((2, FRAMES, parts)),
        pltpu.SemaphoreType.DMA((2, FRAMES, parts)),
        pltpu.SemaphoreType.DMA((2, FRAMES)),
        pltpu.SemaphoreType.DMA((2, FRAMES)),
        pltpu.SemaphoreType.DMA((FRAMES, 2)),
        pltpu.SemaphoreType.DMA((2, columns_of_space)),
        pltpu.SemaphoreType.DMA((2, columns_of_space)),
    ]
    return kernel, scratch


def solution(mesh):
    steps, spaces = mesh.shape["step"], mesh.shape["space"]
    cell_count = float(C * FRAMES * PX * spaces)
    kernel, scratch = make_kernel(steps // 2, spaces, cell_count)

    def local(guesses, noise, timesteps, conv_first, conv_second, time_weight):
        anywhere = pl.BlockSpec(memory_space=pl.ANY)
        scalars = pl.BlockSpec(memory_space=pltpu.SMEM)
        first = conv_first.transpose(0, 2, 1).reshape(27 * C, HID)
        states, changes = pl.pallas_call(
            kernel,
            out_shape=(
                jax.ShapeDtypeStruct((C, FRAMES, PX), F32),
                jax.ShapeDtypeStruct((1,), F32),
            ),
            in_specs=[scalars] + [anywhere] * 5,
            out_specs=(anywhere, scalars),
            scratch_shapes=scratch,
            compiler_params=pltpu.CompilerParams(
                collective_id=0, has_side_effects=True, vmem_limit_bytes=56 * 2**20
            ),
        )(timesteps, guesses[0], noise[0], first, conv_second, time_weight)
        return states[None], changes

    in_specs = (
        P("step", None, None, "space"),
        P("step", None, None, "space"),
        P("step", None),
        P(),
        P(),
        P(),
    )
    out_specs = (P("step", None, None, "space"), P("step"))
    return jax.shard_map(local, mesh=mesh, in_specs=in_specs, out_specs=out_specs, check_vma=False)
```
